128 devices in a mesh: rows: 128 (over z, y, x, core).
Axes of the slice: x: 4, y: 4, z: 4, core: 2. Of those that a mesh axis runs over, the one named last changes fastest.
Arguments:
- right_sides: float32 [8, 128, 128, 64], P(None, 'rows'), may hold values from -6 to 6
- lower_tiles: bfloat16 [8, 128, 16, 128, 128], P(None, 'rows'), may hold values from -0.0625 to 0.0625
- diag_inverse: bfloat16 [8, 128, 128, 128], P(None, 'rows'), may hold values from -1.5 to 1.5, as said below
- tile_columns: int32 [8, 128, 16], P(None, 'rows'), may hold values from 0 to 1023, as said below
- tile_counts: int32 [8, 128], P(None, 'rows'), may hold values from 0 to 16, as said below
- level_sets: int32 [8, 128], replicated, may hold values from 0 to 15, as said below
Outputs:
- solution: bfloat16 [8, 128, 128, 64], P(None, 'rows')
The draws below stay inside these ranges and needn't reach their ends.
Inputs may be any that keep to these rules, and one draw needn't show every extreme that they name: `level_sets`: the block rows of one device (one index d) have pairwise different levels; every level from 0 to 15 has block rows. For k < tile_counts of block row g, tile_columns names a block row of a lower level than g's, and slot 0 names one of level exactly one lower; slots from tile_counts on name arbitrary block rows. `tile_counts`: zero exactly for the block rows of level 0. `diag_inverse`: each tile is the inverse of a diagonal tile of the factor.
All inputs are finite; a program needn't handle non-finite values.
Results may differ from the reference program's by a relative error of at most 0.0053.
Values may be sent and summed in bfloat16 or wider, within the bound.
No kernel may reach another device: no remote copies, remote signals or barrier semaphores. Data moves between devices by JAX's collectives and lax.ppermute only.
A program may use at most 64 MiB of HBM per device.

```python
import jax
import jax.numpy as jnp
from jax import lax

B = 128
R = 64
K = 16
LEVELS = 16
BR_DEV = 8
OWNERS = 128


def level_table(key):
    base = jax.random.fold_in(key, 11)
    level_ids = jnp.arange(LEVELS, dtype=jnp.int32)

    def one_device(device):
        sub = jax.random.fold_in(base, device)
        scores = jax.random.randint(sub, (LEVELS,), 0, 65536) * LEVELS + level_ids
        scores = jnp.where(level_ids == device % LEVELS, 1 << 30, scores)
        ranked = jnp.argsort(-scores, stable=True).astype(jnp.int32)
        chosen = ranked[:BR_DEV]
        shuffle = jax.random.permutation(jax.random.fold_in(sub, 1), BR_DEV)
        return chosen[shuffle]
    table = jax.vmap(one_device)(jnp.arange(OWNERS, dtype=jnp.int32))
    return table.T.astype(jnp.int32)


def sparsity(key):
    flat_levels = level_table(key).reshape(-1)
    total_rows = BR_DEV * OWNERS
    row_ids = jnp.arange(total_rows, dtype=jnp.int32)
    base = jax.random.fold_in(key, 23)

    def one_row(row):
        sub = jax.random.fold_in(base, row)
        level_now = flat_levels[row]
        scores = jax.random.randint(sub, (total_rows,), 0, 4096) * total_rows + row_ids
        forced = jnp.argmax(jnp.where(flat_levels == level_now - 1, scores, -1)).astype(jnp.int32)
        values, picks = lax.top_k(jnp.where(flat_levels < level_now, scores, -1), K)
        picks = jnp.where(values >= 0, picks.astype(jnp.int32), forced)
        col_ids = jnp.concatenate([forced[None], picks[:K - 1]])
        used = jax.random.randint(jax.random.fold_in(sub, 5), (), 1, K + 1)
        used = jnp.where(level_now > 0, used, 0).astype(jnp.int32)
        return (col_ids, used)
    col_ids, used = jax.vmap(one_row)(row_ids)
    return (col_ids.reshape(BR_DEV, OWNERS, K), used.reshape(BR_DEV, OWNERS))


def draw_level_sets(key, part):
    return level_table(key)


def draw_tile_columns(key, part):
    return sparsity(key)[0]


def draw_tile_counts(key, part):
    return sparsity(key)[1]


def draw_diag_inverse(key, part):
    sub = jax.random.fold_in(key, 37)
    diag_part = jnp.exp(jax.random.uniform(jax.random.fold_in(sub, 1), (BR_DEV, OWNERS, B), jnp.float32, jnp.log(0.6), jnp.log(1.4)))
    spread = 0.4 * jax.random.normal(jax.random.fold_in(sub, 2), (BR_DEV, OWNERS, B, B), jnp.float32) / jnp.sqrt(B * 1.0)
    spread = jnp.clip(spread, -1.5, 1.5)
    eye = jnp.eye(B, dtype=jnp.float32)
    return (spread * (1.0 - eye) + diag_part[..., None] * eye).astype(jnp.bfloat16)


def block_levels(own_key, shape, shards, low, top_value):
    loudness = 1.0
    for axis_at, shards_of in shards:
        draws = jax.random.uniform(jax.random.fold_in(jax.random.fold_in(own_key, 6), axis_at), (shards_of,), jnp.float32, low / len(shards), top_value / len(shards))
        loudness = loudness * jnp.repeat(jnp.exp(draws), shape[axis_at] // shards_of).reshape((-1,) + (1,) * (len(shape) - 1 - axis_at))
    return loudness


def gaussian(key, shape, scale, bound, pieces=(), kind=jnp.bfloat16):
    gain = block_levels(key, shape, pieces, -0.22, 0.18) if pieces else 1.0
    drawn = jax.random.normal(key, shape, jnp.float32) * scale * gain
    return jnp.minimum(jnp.maximum(drawn, -bound), bound).astype(kind)


def setup_inputs(seed: int = 0) -> dict:
    splits = jax.random.split(jax.random.key(seed), 7)
    return {
        "right_sides": gaussian(splits[0], (BR_DEV, OWNERS, B, R), 1.0, 6.0, ((1, 128),), jnp.float32),
        "lower_tiles": gaussian(splits[1], (BR_DEV, OWNERS, K, B, B), (4 * B * K) ** -0.5, 0.0625, ((1, 128),)),
        "diag_inverse": draw_diag_inverse(jax.random.fold_in(splits[6], 71), 0),
        "tile_columns": draw_tile_columns(jax.random.fold_in(splits[6], 71), 0),
        "tile_counts": draw_tile_counts(jax.random.fold_in(splits[6], 71), 0),
        "level_sets": draw_level_sets(jax.random.fold_in(splits[6], 71), 0),
    }


def reference(right_sides, lower_tiles, diag_inverse, tile_columns, tile_counts, level_sets):
    total_rows = BR_DEV * OWNERS
    rhs_flat = right_sides.reshape(total_rows, B, R)
    tiles_flat = lower_tiles.reshape(total_rows, K, B, B)
    inverse_flat = diag_inverse.reshape(total_rows, B, B)
    columns_flat = tile_columns.reshape(total_rows, K).astype(jnp.int32)
    counts_flat = tile_counts.reshape(total_rows).astype(jnp.int32)
    levels_flat = level_sets.reshape(total_rows).astype(jnp.int32)
    row_ids = jnp.arange(total_rows, dtype=jnp.int32)
    row_order = jnp.argsort(levels_flat * total_rows + row_ids, stable=True).astype(jnp.int32)
    slot_ids = jnp.arange(K, dtype=jnp.int32)

    def advance(solution, row):
        col_ids = columns_flat[row]
        in_use = slot_ids < counts_flat[row]
        blocks = solution[col_ids].astype(jnp.float32)
        blocks = jnp.where(in_use[:, None, None], blocks, jnp.zeros_like(blocks))
        update = jnp.einsum("kab,kbr->ar", tiles_flat[row].astype(jnp.float32), blocks)
        rounded = (rhs_flat[row] - update).astype(jnp.bfloat16)
        solved = jnp.dot(inverse_flat[row], rounded, preferred_element_type=jnp.float32).astype(jnp.bfloat16)
        return solution.at[row].set(solved), None

    start = jnp.zeros((total_rows, B, R), jnp.bfloat16)
    solution, unused = lax.scan(advance, start, row_order)
    return solution.reshape(BR_DEV, OWNERS, B, R)
```

```python
import functools

import jax
import jax.numpy as jnp
from jax import lax
from jax.experimental import pallas as pl
from jax.experimental.pallas import tpu as pltpu
from jax.sharding import Mesh
from jax.sharding import PartitionSpec as P

LEVELS = 16
ROWS = ("rows_0", "rows_1", "rows_2", "rows_3")
CHIPS = ("rows_0", "rows_1", "rows_2")
CORE = "rows_3"
SWAP = ((0, 1), (1, 0))
MEMBERS = 2
KEYS = LEVELS * 2 * MEMBERS
RING = 8


def smem():
    return pl.BlockSpec(memory_space=pltpu.SMEM)


def vmem():
    return pl.BlockSpec(memory_space=pltpu.VMEM)


def anywhere():
    return pl.BlockSpec(memory_space=pl.ANY)


def bucket(level, urgent, member):
    return (level * 2 + (0 if urgent else 1)) * MEMBERS + member


def times_transposed(rows, tile):
    return lax.dot_general(
        rows, tile, (((1,), (1,)), ((), ())), preferred_element_type=jnp.float32
    )


def list_edges(owners, columns, counts, row_levels, levels, edges, starts, fill):
    members_rows = counts.shape[0] // MEMBERS
    width_k = columns.shape[0] // counts.shape[0]

    def clear(key, unused):
        fill[key] = 0
        return unused

    lax.fori_loop(0, KEYS, clear, 0)

    def key_of(row, slot):
        col = columns[row * width_k + slot]
        level = levels[col]
        late = jnp.where(row_levels[row] == level + 1, 0, 1)
        return col, (level * 2 + late) * MEMBERS + row // members_rows

    def count_row(row, unused):
        def count(slot, unused):
            col, key = key_of(row, slot)
            fill[key] = fill[key] + 1
            return unused

        return lax.fori_loop(0, counts[row], count, unused)

    lax.fori_loop(0, counts.shape[0], count_row, 0)

    def prefix(key, total):
        starts[key] = total
        here = fill[key]
        fill[key] = total
        return total + here

    starts[KEYS] = lax.fori_loop(0, KEYS, prefix, 0)

    def place_row(row, unused):
        def place(slot, unused):
            col, key = key_of(row, slot)
            at = fill[key]
            edges[at] = (row * width_k + slot) * owners + col % owners
            fill[key] = at + 1
            return unused

        return lax.fori_loop(0, counts[row], place, unused)

    lax.fori_loop(0, counts.shape[0], place_row, 0)


def solve_level(level, rows, width_k, owners, core, row_levels, *refs):
    if level:
        edges, starts, received, held, *refs = refs
    else:
        held, *refs = refs
    tiles, inverses = refs[:MEMBERS], refs[MEMBERS : 2 * MEMBERS]
    piece, tile_buf, inverse_buf, tile_sem, inverse_sem = refs[2 * MEMBERS :]

    picked = []
    for member in range(MEMBERS):
        row = jnp.int32(-1)
        for s in range(rows):
            row = jnp.where(row_levels[member * rows + s] == level, s, row)
        picked.append(row)

    def inverse_copy(member):
        return pltpu.make_async_copy(
            inverses[member].at[jnp.maximum(picked[member], 0)],
            inverse_buf.at[member],
            inverse_sem.at[member],
        )

    def tile_copy(member, first, i):
        code = edges[first + i] // owners - member * rows * width_k
        return pltpu.make_async_copy(
            tiles[member].at[code // width_k, code % width_k],
            tile_buf.at[member * width_k + i],
            tile_sem.at[member * width_k + i],
        )

    spans = []
    for member in range(MEMBERS):
        if level:
            first = starts[bucket(level - 1, True, member)]
            spans.append((first, starts[bucket(level - 1, True, member) + 1] - first))

            def begin(i, unused, member=member, first=first):
                tile_copy(member, first, i).start()
                return unused

            lax.fori_loop(0, spans[member][1], begin, 0)

        @pl.when(picked[member] >= 0)
        def _(member=member):
            inverse_copy(member).start()

    for member in range(MEMBERS):
        at = core[0] if member == 0 else 1 - core[0]

        @pl.when(picked[member] < 0)
        def _(at=at):
            piece[at] = jnp.zeros(piece.shape[1:], piece.dtype)

        @pl.when(picked[member] >= 0)
        def _(member=member, at=at):
            total = held[member * rows + picked[member]]
            if level:
                first, many = spans[member]

                def absorb(i, total):
                    tile_copy(member, first, i).wait()
                    block = received[edges[first + i] % owners]
                    return total - times_transposed(block, tile_buf[member * width_k + i])

                total = lax.fori_loop(0, many, absorb, total)
            inverse_copy(member).wait()
            solved = times_transposed(total.astype(jnp.bfloat16), inverse_buf[member])
            piece[at] = solved.astype(jnp.bfloat16)


def absorb_level(level, rows, width_k, owners, edges, starts, received, held_in, *refs):
    tiles, (held, tile_buf, tile_sem) = refs[:MEMBERS], refs[MEMBERS:]
    held[...] = held_in[...]
    for member in range(MEMBERS):
        first = starts[bucket(level - 1, False, member)]
        many = starts[bucket(level - 1, False, member) + 1] - first

        def tile_copy(i, member=member, first=first):
            code = edges[first + i] // owners - member * rows * width_k
            at = lax.rem(i, RING)
            return pltpu.make_async_copy(
                tiles[member].at[code // width_k, code % width_k],
                tile_buf.at[at],
                tile_sem.at[at],
            )

        def begin(i, unused, tile_copy=tile_copy):
            tile_copy(i).start()
            return unused

        lax.fori_loop(0, jnp.minimum(many, RING), begin, 0)

        def absorb(i, unused, tile_copy=tile_copy, first=first, many=many):
            tile_copy(i).wait()
            code = edges[first + i]
            row = code // (owners * width_k)
            given = times_transposed(received[code % owners], tile_buf[lax.rem(i, RING)])
            held[row] = held[row] - given

            @pl.when(i + RING < many)
            def _():
                tile_copy(i + RING).start()

            return unused

        lax.fori_loop(0, many, absorb, 0)


def local(right_sides, lower_tiles, diag_inverse, tile_columns, tile_counts, level_sets):
    owners = lax.axis_size(ROWS)
    chips = lax.axis_size(CHIPS)
    own_index = lax.axis_index(ROWS)
    core = lax.axis_index(CORE)
    rows, unused_one, width_k = tile_columns.shape
    part = right_sides.shape[3] // MEMBERS
    lanes = right_sides.shape[2]

    def swapped(value):
        return lax.ppermute(value, CORE, SWAP)

    rhs = jnp.swapaxes(right_sides[:, 0], 1, 2)
    rhs_mine = lax.dynamic_slice_in_dim(rhs, core * part, part, 1)
    rhs_theirs = swapped(lax.dynamic_slice_in_dim(rhs, (1 - core) * part, part, 1))
    held = jnp.concatenate([rhs_mine, rhs_theirs])
    inverses = (diag_inverse[:, 0], swapped(diag_inverse[:, 0]))
    tiles = (lower_tiles[:, 0], swapped(lower_tiles[:, 0]))
    columns = jnp.concatenate([tile_columns[:, 0].reshape(-1), swapped(tile_columns[:, 0]).reshape(-1)])
    counts = jnp.concatenate([tile_counts[:, 0], swapped(tile_counts[:, 0])])
    levels_of = lambda device: lax.dynamic_slice_in_dim(level_sets, device, 1, 1)[:, 0]
    row_levels = jnp.concatenate(
        [levels_of(own_index), levels_of(own_index + 1 - 2 * core)]
    )
    core_id = core.reshape(1).astype(jnp.int32)

    edges, starts = pl.pallas_call(
        functools.partial(list_edges, owners),
        out_shape=(
            jax.ShapeDtypeStruct((columns.size,), jnp.int32),
            jax.ShapeDtypeStruct((KEYS + 1,), jnp.int32),
        ),
        in_specs=[smem()] * 4,
        out_specs=(smem(), smem()),
        scratch_shapes=[pltpu.SMEM((KEYS,), jnp.int32)],
        name="list_edges",
    )(columns, counts, row_levels, level_sets.reshape(-1))

    block = (part, lanes)
    tile = lower_tiles.shape[3:]

    def solve(level, received, held):
        lists = ((edges, starts, received) if level else ()) + (held,)
        return pl.pallas_call(
            functools.partial(solve_level, level, rows, width_k, owners),
            out_shape=jax.ShapeDtypeStruct((MEMBERS, *block), jnp.bfloat16),
            in_specs=[smem(), smem()]
            + ([smem(), smem(), vmem()] if level else [])
            + [vmem()]
            + [anywhere()] * (2 * MEMBERS),
            out_specs=vmem(),
            scratch_shapes=[
                pltpu.VMEM((MEMBERS * width_k, *tile), jnp.bfloat16),
                pltpu.VMEM((MEMBERS, *tile), jnp.bfloat16),
                pltpu.SemaphoreType.DMA((MEMBERS * width_k,)),
                pltpu.SemaphoreType.DMA((MEMBERS,)),
            ],
            compiler_params=pltpu.CompilerParams(vmem_limit_bytes=8 << 20),
            cost_estimate=pl.CostEstimate(flops=4 << 20, bytes_accessed=1 << 18, transcendentals=0),
            name=f"solve_{level}",
        )(core_id, row_levels, *lists, *tiles, *inverses)

    def absorb(level, received, held):
        return pl.pallas_call(
            functools.partial(absorb_level, level, rows, width_k, owners),
            out_shape=jax.ShapeDtypeStruct(held.shape, held.dtype),
            in_specs=[smem(), smem(), vmem(), vmem()] + [anywhere()] * MEMBERS,
            out_specs=vmem(),
            scratch_shapes=[
                pltpu.VMEM((RING, *tile), jnp.bfloat16),
                pltpu.SemaphoreType.DMA((RING,)),
            ],
            compiler_params=pltpu.CompilerParams(vmem_limit_bytes=8 << 20),
            cost_estimate=pl.CostEstimate(flops=32 << 20, bytes_accessed=1 << 20, transcendentals=0),
            name=f"absorb_{level}",
        )(edges, starts, received, held, *tiles)

    received = None
    pieces = []
    for level in range(LEVELS):
        piece = solve(level, received, held)
        pieces.append(piece)
        if level == LEVELS - 1:
            break
        arriving = lax.all_to_all(
            jnp.broadcast_to(piece[None], (chips, *piece.shape)), CHIPS, 0, 0, tiled=True
        )
        if level:
            held = absorb(level, received, held)
        received = arriving.reshape(owners, *block)

    pieces = jnp.stack(pieces)
    mine = pieces[row_levels[:rows], core]
    theirs = swapped(pieces[row_levels[rows:], 1 - core])
    both = jnp.concatenate([mine, theirs], 1)
    crossed = jnp.concatenate([theirs, mine], 1)
    return jnp.swapaxes(jnp.where(core == 0, both, crossed), 1, 2)[:, None]


def solution(mesh):
    finer = Mesh(mesh.devices.reshape(4, 4, 4, 2), ROWS)
    return jax.shard_map(
        local,
        mesh=finer,
        in_specs=(
            P(None, ROWS, None, None),
            P(None, ROWS, None, None, None),
            P(None, ROWS, None, None),
            P(None, ROWS, None),
            P(None, ROWS),
            P(),
        ),
        out_specs=P(None, ROWS, None, None),
        check_vma=False,
    )
```

```python
import functools

import jax
import jax.numpy as jnp
from jax import lax
from jax.experimental import pallas as pl
from jax.experimental.pallas import tpu as pltpu
from jax.sharding import Mesh
from jax.sharding import PartitionSpec as P

LEVELS = 16
ROWS = ("rows_0", "rows_1", "rows_2", "rows_3")
CHIPS = ("rows_0", "rows_1", "rows_2")
CORE = "rows_3"
SWAP = ((0, 1), (1, 0))
MEMBERS = 2
KEYS = LEVELS * 2 * MEMBERS
RING = 8


def smem():
    return pl.BlockSpec(memory_space=pltpu.SMEM)


def vmem():
    return pl.BlockSpec(memory_space=pltpu.VMEM)


def anywhere():
    return pl.BlockSpec(memory_space=pltpu.HBM)


def bucket(level, urgent, member):
    return (level * 2 + (0 if urgent else 1)) * MEMBERS + member


def times_transposed(rows, tile):
    return lax.dot_general(
        rows, tile, (((1,), (1,)), ((), ())), preferred_element_type=jnp.float32
    )


def list_edges(owners, columns, counts, row_levels, levels, edges, starts, fill):
    members_rows = counts.shape[0] // MEMBERS
    width_k = columns.shape[0] // counts.shape[0]

    def clear(key, unused):
        fill[key] = 0
        return unused

    lax.fori_loop(0, KEYS, clear, 0)

    def key_of(row, slot):
        col = columns[row * width_k + slot]
        level = levels[col]
        late = jnp.where(row_levels[row] == level + 1, 0, 1)
        return col, (level * 2 + late) * MEMBERS + row // members_rows

    def count_row(row, unused):
        def count(slot, unused):
            col, key = key_of(row, slot)
            fill[key] = fill[key] + 1
            return unused

        return lax.fori_loop(0, counts[row], count, unused)

    lax.fori_loop(0, counts.shape[0], count_row, 0)

    def prefix(key, total):
        starts[key] = total
        here = fill[key]
        fill[key] = total
        return total + here

    starts[KEYS] = lax.fori_loop(0, KEYS, prefix, 0)

    def place_row(row, unused):
        def place(slot, unused):
            col, key = key_of(row, slot)
            at = fill[key]
            edges[at] = (row * width_k + slot) * owners + col % owners
            fill[key] = at + 1
            return unused

        return lax.fori_loop(0, counts[row], place, unused)

    lax.fori_loop(0, counts.shape[0], place_row, 0)


def solve_level(level, rows, width_k, owners, core, row_levels, *refs):
    if level:
        edges, starts, received, held, *refs = refs
    else:
        held, *refs = refs
    tiles, inverses = refs[:MEMBERS], refs[MEMBERS : 2 * MEMBERS]
    piece, tile_buf, inverse_buf, tile_sem, inverse_sem = refs[2 * MEMBERS :]

    picked = []
    for member in range(MEMBERS):
        row = jnp.int32(-1)
        for s in range(rows):
            row = jnp.where(row_levels[member * rows + s] == level, s, row)
        picked.append(row)

    def inverse_copy(member):
        return pltpu.make_async_copy(
            inverses[member].at[jnp.maximum(picked[member], 0)],
            inverse_buf.at[member],
            inverse_sem.at[member],
        )

    def tile_copy(member, first, i):
        code = edges[first + i] // owners - member * rows * width_k
        return pltpu.make_async_copy(
            tiles[member].at[code // width_k, code % width_k],
            tile_buf.at[member * width_k + i],
            tile_sem.at[member * width_k + i],
        )

    spans = []
    for member in range(MEMBERS):
        if level:
            first = starts[bucket(level - 1, True, member)]
            spans.append((first, starts[bucket(level - 1, True, member) + 1] - first))

            def begin(i, unused, member=member, first=first):
                tile_copy(member, first, i).start()
                return unused

            lax.fori_loop(0, spans[member][1], begin, 0)

        @pl.when(picked[member] >= 0)
        def _(member=member):
            inverse_copy(member).start()

    for member in range(MEMBERS):
        at = core[0] if member == 0 else 1 - core[0]

        @pl.when(picked[member] < 0)
        def _(at=at):
            piece[at] = jnp.zeros(piece.shape[1:], piece.dtype)

        @pl.when(picked[member] >= 0)
        def _(member=member, at=at):
            total = held[member * rows + picked[member]]
            if level:
                first, many = spans[member]

                def absorb(i, total):
                    tile_copy(member, first, i).wait()
                    block = received[edges[first + i] % owners]
                    return total - times_transposed(block, tile_buf[member * width_k + i])

                total = lax.fori_loop(0, many, absorb, total)
            inverse_copy(member).wait()
            solved = times_transposed(total.astype(jnp.bfloat16), inverse_buf[member])
            piece[at] = solved.astype(jnp.bfloat16)


def absorb_level(level, rows, width_k, owners, edges, starts, received, held_in, *refs):
    tiles, (held, tile_buf, tile_sem) = refs[:MEMBERS], refs[MEMBERS:]
    held[...] = held_in[...]
    for member in range(MEMBERS):
        first = starts[bucket(level - 1, False, member)]
        many = starts[bucket(level - 1, False, member) + 1] - first

        def tile_copy(i, member=member, first=first):
            code = edges[first + i] // owners - member * rows * width_k
            at = lax.rem(i, RING)
            return pltpu.make_async_copy(
                tiles[member].at[code // width_k, code % width_k],
                tile_buf.at[at],
                tile_sem.at[at],
            )

        def begin(i, unused, tile_copy=tile_copy):
            tile_copy(i).start()
            return unused

        lax.fori_loop(0, jnp.minimum(many, RING), begin, 0)

        def absorb(i, unused, tile_copy=tile_copy, first=first, many=many):
            tile_copy(i).wait()
            code = edges[first + i]
            row = code // (owners * width_k)
            given = times_transposed(received[code % owners], tile_buf[lax.rem(i, RING)])
            held[row] = held[row] - given

            @pl.when(i + RING < many)
            def _():
                tile_copy(i + RING).start()

            return unused

        lax.fori_loop(0, many, absorb, 0)


def collect_rows(rows, core, row_levels, *refs):
    pieces, outs = refs[:LEVELS], refs[LEVELS:]
    for level in range(LEVELS):
        for member in range(MEMBERS):
            at = core[0] if member == 0 else 1 - core[0]
            for s in range(rows):

                @pl.when(row_levels[member * rows + s] == level)
                def _(level=level, member=member, at=at, s=s):
                    outs[member][s] = pieces[level][at]


def local(right_sides, lower_tiles, diag_inverse, tile_columns, tile_counts, level_sets):
    owners = lax.axis_size(ROWS)
    chips = lax.axis_size(CHIPS)
    own_index = lax.axis_index(ROWS)
    core = lax.axis_index(CORE)
    rows, unused_one, width_k = tile_columns.shape
    part = right_sides.shape[3] // MEMBERS
    lanes = right_sides.shape[2]

    def swapped(value):
        return lax.ppermute(value, CORE, SWAP)

    rhs = jnp.swapaxes(right_sides[:, 0], 1, 2)
    rhs_mine = lax.dynamic_slice_in_dim(rhs, core * part, part, 1)
    rhs_theirs = swapped(lax.dynamic_slice_in_dim(rhs, (1 - core) * part, part, 1))
    held = jnp.concatenate([rhs_mine, rhs_theirs])
    inverses = (diag_inverse[:, 0], swapped(diag_inverse[:, 0]))
    tiles = (lower_tiles[:, 0], swapped(lower_tiles[:, 0]))
    columns = jnp.concatenate([tile_columns[:, 0].reshape(-1), swapped(tile_columns[:, 0]).reshape(-1)])
    counts = jnp.concatenate([tile_counts[:, 0], swapped(tile_counts[:, 0])])
    levels_of = lambda device: lax.dynamic_slice_in_dim(level_sets, device, 1, 1)[:, 0]
    row_levels = jnp.concatenate(
        [levels_of(own_index), levels_of(own_index + 1 - 2 * core)]
    )
    core_id = core.reshape(1).astype(jnp.int32)

    edges, starts = pl.pallas_call(
        functools.partial(list_edges, owners),
        out_shape=(
            jax.ShapeDtypeStruct((columns.size,), jnp.int32),
            jax.ShapeDtypeStruct((KEYS + 1,), jnp.int32),
        ),
        in_specs=[smem()] * 4,
        out_specs=(smem(), smem()),
        scratch_shapes=[pltpu.SMEM((KEYS,), jnp.int32)],
        name="list_edges",
    )(columns, counts, row_levels, level_sets.reshape(-1))

    block = (part, lanes)
    tile = lower_tiles.shape[3:]

    def solve(level, received, held):
        lists = ((edges, starts, received) if level else ()) + (held,)
        return pl.pallas_call(
            functools.partial(solve_level, level, rows, width_k, owners),
            out_shape=jax.ShapeDtypeStruct((MEMBERS, *block), jnp.bfloat16),
            in_specs=[smem(), smem()]
            + ([smem(), smem(), vmem()] if level else [])
            + [vmem()]
            + [anywhere()] * (2 * MEMBERS),
            out_specs=vmem(),
            scratch_shapes=[
                pltpu.VMEM((MEMBERS * width_k, *tile), jnp.bfloat16),
                pltpu.VMEM((MEMBERS, *tile), jnp.bfloat16),
                pltpu.SemaphoreType.DMA((MEMBERS * width_k,)),
                pltpu.SemaphoreType.DMA((MEMBERS,)),
            ],
            compiler_params=pltpu.CompilerParams(vmem_limit_bytes=52 << 20),
            cost_estimate=pl.CostEstimate(flops=4 << 20, bytes_accessed=1 << 18, transcendentals=0),
            name=f"solve_{level}",
        )(core_id, row_levels, *lists, *tiles, *inverses)

    def absorb(level, received, held):
        return pl.pallas_call(
            functools.partial(absorb_level, level, rows, width_k, owners),
            out_shape=jax.ShapeDtypeStruct(held.shape, held.dtype),
            in_specs=[smem(), smem(), vmem(), vmem()] + [anywhere()] * MEMBERS,
            out_specs=vmem(),
            scratch_shapes=[
                pltpu.VMEM((RING, *tile), jnp.bfloat16),
                pltpu.SemaphoreType.DMA((RING,)),
            ],
            compiler_params=pltpu.CompilerParams(vmem_limit_bytes=52 << 20),
            cost_estimate=pl.CostEstimate(flops=32 << 20, bytes_accessed=1 << 20, transcendentals=0),
            name=f"absorb_{level}",
        )(edges, starts, received, held, *tiles)

    received = None
    pieces = []
    for level in range(LEVELS):
        piece = solve(level, received, held)
        pieces.append(piece)
        if level == LEVELS - 1:
            break
        arriving = lax.all_to_all(
            jnp.broadcast_to(piece[None], (chips, *piece.shape)), CHIPS, 0, 0, tiled=True
        )
        if level:
            held = absorb(level, received, held)
        received = arriving.reshape(owners, *block)

    mine, theirs = pl.pallas_call(
        functools.partial(collect_rows, rows),
        out_shape=(jax.ShapeDtypeStruct((rows, *block), jnp.bfloat16),) * MEMBERS,
        in_specs=[smem(), smem()] + [vmem()] * LEVELS,
        out_specs=(vmem(),) * MEMBERS,
        compiler_params=pltpu.CompilerParams(vmem_limit_bytes=52 << 20),
        name="collect_rows",
    )(core_id, row_levels, *pieces)
    theirs = swapped(theirs)
    both = jnp.concatenate([mine, theirs], 1)
    crossed = jnp.concatenate([theirs, mine], 1)
    return jnp.swapaxes(jnp.where(core == 0, both, crossed), 1, 2)[:, None]


def solution(mesh):
    finer = Mesh(mesh.devices.reshape(4, 4, 4, 2), ROWS)
    return jax.shard_map(
        local,
        mesh=finer,
        in_specs=(
            P(None, ROWS, None, None),
            P(None, ROWS, None, None, None),
            P(None, ROWS, None, None),
            P(None, ROWS, None),
            P(None, ROWS),
            P(),
        ),
        out_specs=P(None, ROWS, None, None),
        check_vma=False,
    )
```

```python
import functools

import jax
import jax.numpy as jnp
from jax import lax
from jax.experimental import pallas as pl
from jax.experimental.pallas import tpu as pltpu
from jax.sharding import Mesh
from jax.sharding import PartitionSpec as P

LEVELS = 16
ROWS = ("rows_0", "rows_1", "rows_2", "rows_3")
LINE = "rows_2"
REST = ("rows_0", "rows_1", "rows_3")
GRANT = 52 << 20


def smem():
    return pl.BlockSpec(memory_space=pltpu.SMEM)


def vmem():
    return pl.BlockSpec(memory_space=pltpu.VMEM)


def hbm():
    return pl.BlockSpec(memory_space=pltpu.HBM)


def kernel_params(vmem_limit=GRANT):
    return pltpu.CompilerParams(vmem_limit_bytes=vmem_limit)


def times_transposed(rows, tile):
    return lax.dot_general(
        rows, tile, (((1,), (1,)), ((), ())), preferred_element_type=jnp.float32
    )


def solve_first(owners, ids, levels, rhs, inverse, piece, inverse_buf, rhs_buf, sems):
    rows = rhs.shape[0]
    members, part, lanes = piece.shape
    pick = jnp.int32(-1)
    for s in range(rows):
        pick = jnp.where(levels[s * owners + ids[0]] == 0, s, pick)

    @pl.when(pick < 0)
    def _():
        piece[...] = jnp.zeros(piece.shape, piece.dtype)

    @pl.when(pick >= 0)
    def _():
        copies = (
            pltpu.make_async_copy(inverse.at[pick], inverse_buf, sems.at[0]),
            pltpu.make_async_copy(rhs.at[pick], rhs_buf, sems.at[1]),
        )
        for copy in copies:
            copy.start()
        for copy in copies:
            copy.wait()
        solved = times_transposed(rhs_buf[...].astype(jnp.bfloat16), inverse_buf[...])
        piece[...] = solved.astype(jnp.bfloat16).reshape(piece.shape)


def prepare_level(level, members, rows, width_k, owners, ranks, cut, *refs):
    ids, levels, columns, counts, rhs, own_tiles, own_inverse = refs[:7]
    refs = refs[7:]
    near, far_side, low, high = (refs[i * ranks : (i + 1) * ranks] for i in range(4))
    refs = refs[4 * ranks :]
    late_part = level >= 2
    if late_part:
        received, *refs = refs
        if level >= 3:
            unused_store, *refs = refs
    acc, tiles, info, places, *refs = refs
    if late_part:
        store, *refs = refs
    tile_sem, x_sem, put_sem, x_buf, sources = refs
    slots = 1 + width_k

    if late_part:
        put = pltpu.make_async_copy(received, store.at[level - 2], put_sem.at[0])
        put.start()

    def begin(member, row, rank, t, place):
        def go(source):
            pltpu.make_async_copy(
                source, tiles.at[member, place], tile_sem.at[member * slots + place]
            ).start()

        if member == 0:
            if isinstance(t, int):
                go(own_inverse.at[row])
            else:
                go(own_tiles.at[row, t - 1])
            return
        for r in range(ranks):

            @pl.when(rank == r)
            def _(r=r):
                if member == 1:
                    go(near[r].at[t])
                elif member == 3:
                    go(far_side[r].at[t])
                elif isinstance(t, int):
                    go(low[r].at[t])
                else:

                    @pl.when(t < cut)
                    def _():
                        go(low[r].at[t])

                    @pl.when(t >= cut)
                    def _():
                        go(high[r].at[t - cut])

    def wait_tile(member, place):
        pltpu.make_async_copy(
            own_inverse.at[0], tiles.at[member, place], tile_sem.at[member * slots + place]
        ).wait()

    def x_copy(at):
        return pltpu.make_async_copy(
            store.at[sources[at] // owners, lax.rem(sources[at], owners)],
            x_buf.at[at],
            x_sem.at[at],
        )

    found = []
    for member in range(members):
        device = ids[member]
        pick = jnp.int32(-1)
        rank = jnp.int32(0)
        for s in range(rows):
            here = levels[s * owners + device]
            pick = jnp.where(here == level, s, pick)
            rank = rank + jnp.where((here >= 1) & (here < level), 1, 0)
        row = jnp.maximum(pick, 0)
        many = jnp.where(pick >= 0, counts[member * rows + row], 0)

        @pl.when(pick >= 0)
        def _(member=member, row=row, rank=rank):
            begin(member, row, rank, 0, 0)

        def scan(k, tally, member=member, row=row, rank=rank):
            late, urgent = tally
            col = columns[(member * rows + row) * width_k + k]
            source = levels[col]
            device = lax.rem(col, owners)
            place = (device // 8 * 2 + lax.rem(device, 2)) * members + lax.rem(device // 2, members)
            place = jnp.where(source == 0, device, place)
            is_urgent = source == level - 1
            begin(member, row, rank, k + 1, jnp.where(is_urgent, 1 + urgent, width_k - late))

            @pl.when(is_urgent)
            def _():
                places[member * width_k + urgent] = place

            @pl.when(jnp.logical_not(is_urgent))
            def _():
                sources[member * width_k + late] = source * owners + place

            step = jnp.where(is_urgent, 1, 0)
            return late + 1 - step, urgent + step

        late, urgent = lax.fori_loop(0, many, scan, (jnp.int32(0), jnp.int32(0)))
        info[member] = urgent
        info[members + member] = jnp.where(pick >= 0, 1, 0)
        found.append((pick, row, late, urgent))

    if late_part:
        put.wait()
        for member in range(members):

            def fetch(i, unused, member=member):
                x_copy(member * width_k + i).start()
                return unused

            lax.fori_loop(0, found[member][2], fetch, 0)

    for member in range(members):
        pick, row, late, urgent = found[member]
        total = rhs[member, row]
        if late_part:

            def absorb(i, total, member=member):
                x_copy(member * width_k + i).wait()
                wait_tile(member, width_k - i)
                return total - times_transposed(
                    x_buf[member * width_k + i], tiles[member, width_k - i]
                )

            total = lax.fori_loop(0, late, absorb, total)
        acc[member] = total

    for member in range(members):
        pick, row, late, urgent = found[member]

        @pl.when(pick >= 0)
        def _(member=member):
            wait_tile(member, 0)

        def settle(i, unused, member=member):
            wait_tile(member, 1 + i)
            return unused

        lax.fori_loop(0, urgent, settle, 0)


def solve_level(members, width_k, ids, info, places, acc, tiles, received, piece):
    for member in range(members):
        at = ids[members + member]

        @pl.when(info[members + member] == 0)
        def _(at=at):
            piece[at] = jnp.zeros(piece.shape[1:], piece.dtype)

        @pl.when(info[members + member] > 0)
        def _(member=member, at=at):
            def absorb(i, total):
                block = received[places[member * width_k + i]]
                return total - times_transposed(block, tiles[member, 1 + i])

            total = lax.fori_loop(0, info[member], absorb, acc[member])
            solved = times_transposed(total.astype(jnp.bfloat16), tiles[member, 0])
            piece[at] = solved.astype(jnp.bfloat16)


def collect_rows(members, rows, owners, ids, levels, *refs):
    pieces, outs = refs[: LEVELS - 1], refs[LEVELS - 1 :]
    for member in range(members):
        at = ids[members + member]
        for s in range(rows):
            here = levels[s * owners + ids[member]]
            for level in range(1, LEVELS):

                @pl.when(here == level)
                def _(level=level, member=member, at=at, s=s):
                    outs[member][s] = pieces[level - 1][at]


def local(right_sides, lower_tiles, diag_inverse, tile_columns, tile_counts, level_sets):
    owners = lax.axis_size(ROWS)
    members = lax.axis_size(LINE)
    rest = lax.axis_size(REST)
    own_index = lax.axis_index(ROWS)
    x = lax.axis_index(LINE)
    rows, unused_one, width_k = tile_columns.shape
    lanes, width = right_sides.shape[2:]
    part = width // members
    block = (part, lanes)
    tile = lower_tiles.shape[3:]
    cut = (width_k + 2) // 2

    def shifted(value, shift):
        return lax.ppermute(value, LINE, [(i, (i + shift) % members) for i in range(members)])

    member_x = [lax.rem(x + members - m, members) for m in range(members)]
    ids = jnp.stack([own_index + 2 * (mx - x) for mx in member_x] + member_x).astype(jnp.int32)
    levels = level_sets.reshape(-1)
    own_levels = lax.dynamic_slice_in_dim(level_sets, own_index, 1, 1)[:, 0]

    rhs = jnp.swapaxes(right_sides[:, 0], 1, 2)
    tiles = lower_tiles[:, 0]
    inverse = diag_inverse[:, 0]

    first = pl.pallas_call(
        functools.partial(solve_first, owners),
        out_shape=jax.ShapeDtypeStruct((members, *block), jnp.bfloat16),
        in_specs=[smem(), smem(), hbm(), hbm()],
        out_specs=vmem(),
        scratch_shapes=[
            pltpu.VMEM(tile, jnp.bfloat16),
            pltpu.VMEM((width, lanes), jnp.float32),
            pltpu.SemaphoreType.DMA((2,)),
        ],
        compiler_params=kernel_params(),
        name="solve_0",
    )(ids, levels, rhs, inverse)

    key = jnp.where(own_levels == 0, LEVELS, own_levels)
    rank_of = jnp.sum((key[None, :] < key[:, None]).astype(jnp.int32), axis=1)
    row_ids = jnp.arange(rows, dtype=jnp.int32)

    def chunk_of(rank, tie):
        row = jnp.sum(jnp.where(rank_of == rank, row_ids, 0))
        if tie is not None:
            row, unused_tie = lax.optimization_barrier((row, tie))
        return jnp.concatenate(
            [
                lax.dynamic_slice_in_dim(inverse, row, 1, 0),
                lax.dynamic_slice_in_dim(tiles, row, 1, 0)[0],
            ]
        )

    near, far_side, low, high = [], [], [], []

    def send_chunk(rank, tie):
        chunk = chunk_of(rank, tie)
        near.append(shifted(chunk, 1))
        far_side.append(shifted(chunk, members - 1))

    def pass_on(rank, tie):
        up, down = near[rank][:cut], far_side[rank][cut:]
        low.append(shifted(up, 1))
        high.append(shifted(down, members - 1))

    send_chunk(0, None)

    rhs_parts = rhs.reshape(rows, members, part, lanes)
    rhs_for = lambda to: lax.dynamic_slice_in_dim(rhs_parts, to, 1, 1)[:, 0]
    rhs_all = jnp.stack(
        [rhs_for(x)]
        + [shifted(rhs_for(lax.rem(x + m, members)), m) for m in range(1, members)]
    )
    own_meta = jnp.concatenate([tile_columns[:, 0], tile_counts[:, 0, None].repeat(width_k, 1)])
    metas = [own_meta] + [shifted(own_meta, m) for m in range(1, members)]
    columns = jnp.concatenate([meta[:rows].reshape(-1) for meta in metas])
    counts = jnp.concatenate([meta[rows:, 0] for meta in metas])

    def prepare(level, received, store):
        ranks = min(level, rows)
        late_part = level >= 2
        operands = [ids, levels, columns, counts, rhs_all, tiles, inverse]
        operands += near[:ranks] + far_side[:ranks] + low[:ranks] + high[:ranks]
        specs = [smem()] * 4 + [vmem()] + [hbm()] * (2 + 4 * ranks)
        out_shape = [
            jax.ShapeDtypeStruct((members, *block), jnp.float32),
            jax.ShapeDtypeStruct((members, 1 + width_k, *tile), jnp.bfloat16),
            jax.ShapeDtypeStruct((2 * members,), jnp.int32),
            jax.ShapeDtypeStruct((members * width_k,), jnp.int32),
        ]
        out_specs = [vmem(), vmem(), smem(), smem()]
        aliases = {}
        if late_part:
            operands.append(received)
            specs.append(vmem())
            if level >= 3:
                aliases = {len(operands): len(out_shape)}
                operands.append(store)
                specs.append(hbm())
            out_shape.append(
                jax.ShapeDtypeStruct((LEVELS - 2, owners, *block), jnp.bfloat16)
            )
            out_specs.append(hbm())
        return pl.pallas_call(
            functools.partial(prepare_level, level, members, rows, width_k, owners, ranks, cut),
            out_shape=tuple(out_shape),
            in_specs=specs,
            out_specs=tuple(out_specs),
            scratch_shapes=[
                pltpu.SemaphoreType.DMA((members * (1 + width_k),)),
                pltpu.SemaphoreType.DMA((members * width_k,)),
                pltpu.SemaphoreType.DMA((1,)),
                pltpu.VMEM((members * width_k, *block), jnp.bfloat16),
                pltpu.SMEM((members * width_k,), jnp.int32),
            ],
            input_output_aliases=aliases,
            compiler_params=kernel_params(),
            cost_estimate=pl.CostEstimate(flops=16 << 20, bytes_accessed=4 << 20, transcendentals=0),
            name=f"prepare_{level}",
        )(*operands)

    def solve(prepared, received):
        acc, ready, info, places = prepared
        return pl.pallas_call(
            functools.partial(solve_level, members, width_k),
            out_shape=jax.ShapeDtypeStruct((members, *block), jnp.bfloat16),
            in_specs=[smem()] * 3 + [vmem()] * 3,
            out_specs=vmem(),
            compiler_params=kernel_params(),
            cost_estimate=pl.CostEstimate(flops=4 << 20, bytes_accessed=1 << 18, transcendentals=0),
            name="solve_level",
        )(ids, info, places, acc, ready, received)

    spread = (*(lax.axis_size(name) for name in ROWS[:2]), members, lax.axis_size(ROWS[3]))
    arriving = lax.all_to_all(
        jnp.broadcast_to(first[None, None, :, None], (*spread, *block)).reshape(owners, *block),
        ROWS,
        0,
        0,
        tiled=True,
    )
    pieces = []
    received, store, piece = None, None, first
    for level in range(1, LEVELS):
        rank = level - 1
        if rank < rows:
            pass_on(rank, piece)
            if rank + 1 < rows:
                send_chunk(rank + 1, piece)
        acc, ready, info, places, *kept = prepare(level, received, store)
        if kept:
            store = kept[0]
        received = arriving
        piece = solve((acc, ready, info, places), received)
        pieces.append(piece)
        if level < LEVELS - 1:
            arriving = lax.all_to_all(
                jnp.broadcast_to(piece[None], (rest, *piece.shape)), REST, 0, 0, tiled=True
            ).reshape(owners, *block)

    outs = pl.pallas_call(
        functools.partial(collect_rows, members, rows, owners),
        out_shape=(jax.ShapeDtypeStruct((rows, *block), jnp.bfloat16),) * members,
        in_specs=[smem(), smem()] + [vmem()] * (LEVELS - 1),
        out_specs=(vmem(),) * members,
        compiler_params=kernel_params(),
        name="collect_rows",
    )(ids, levels, *pieces)
    back = [outs[0]] + [shifted(outs[m], members - m) for m in range(1, members)]
    turned = jnp.concatenate(back + back[:-1]).reshape(2 * members - 1, rows, *block)
    turned = lax.dynamic_slice_in_dim(turned, lax.rem(members - x, members), members, 0)
    solved = jnp.where(
        (own_levels == 0)[None, :, None, None], first[:, None], turned
    )
    solved = jnp.swapaxes(solved, 0, 1).reshape(rows, width, lanes)
    return jnp.swapaxes(solved, 1, 2)[:, None]


def solution(mesh):
    finer = Mesh(mesh.devices.reshape(4, 4, 4, 2), ROWS)
    return jax.shard_map(
        local,
        mesh=finer,
        in_specs=(
            P(None, ROWS, None, None),
            P(None, ROWS, None, None, None),
            P(None, ROWS, None, None),
            P(None, ROWS, None),
            P(None, ROWS),
            P(),
        ),
        out_specs=P(None, ROWS, None, None),
        check_vma=False,
    )
```

```python
import functools

import jax
import jax.numpy as jnp
from jax import lax
from jax.experimental import pallas as pl
from jax.experimental.pallas import tpu as pltpu
from jax.sharding import Mesh
from jax.sharding import PartitionSpec as P

LEVELS = 16
ROWS = ("rows_0", "rows_1", "rows_2", "rows_3")
CHIPS = ("rows_0", "rows_1", "rows_2")
CORE = "rows_3"
SWAP = ((0, 1), (1, 0))
MEMBERS = 2
KEYS = LEVELS * 2 * MEMBERS
RING = 8
GROUP = 3
READY = 6
GRANT = 50 << 20


def smem():
    return pl.BlockSpec(memory_space=pltpu.SMEM)


def vmem():
    return pl.BlockSpec(memory_space=pltpu.VMEM)


def anywhere():
    return pl.BlockSpec(memory_space=pltpu.HBM)


def bucket(level, urgent, member):
    return (level * 2 + (0 if urgent else 1)) * MEMBERS + member


def times_transposed(rows, tile):
    return lax.dot_general(
        rows, tile, (((1,), (1,)), ((), ())), preferred_element_type=jnp.float32
    )


def device_of(member, owners_index):
    core = lax.axis_index(CORE)
    return owners_index + (1 - 2 * core) * member


def slot_of(member):
    core = lax.axis_index(CORE)
    return core if member == 0 else 1 - core


def find_row(levels, owners, member, rows, level):
    own = device_of(member, lax.axis_index(ROWS))
    pick = jnp.int32(-1)
    for s in range(rows):
        pick = jnp.where(levels[s * owners + own] == level, s, pick)
    return pick


def list_edges(owners, columns, counts, levels, edges, starts, fill):
    rows = counts.shape[0] // MEMBERS
    width_k = columns.shape[0] // counts.shape[0]

    def clear(key, unused):
        fill[key] = 0
        return unused

    lax.fori_loop(0, KEYS, clear, 0)

    def over_slots(visit):
        for member in range(MEMBERS):
            own = device_of(member, lax.axis_index(ROWS))

            def each_row(row, unused, member=member, own=own):
                next_level = levels[row * owners + own]
                at = member * rows + row

                def each_slot(slot, unused):
                    col = columns[at * width_k + slot]
                    level = levels[col]
                    late = jnp.where(next_level == level + 1, 0, 1)
                    visit(at * width_k + slot, col, (level * 2 + late) * MEMBERS + member)
                    return unused

                return lax.fori_loop(0, counts[at], each_slot, unused)

            lax.fori_loop(0, rows, each_row, 0)

    def count(slot, col, key):
        fill[key] = fill[key] + 1

    over_slots(count)

    def prefix(key, total):
        starts[key] = total
        here = fill[key]
        fill[key] = total
        return total + here

    starts[KEYS] = lax.fori_loop(0, KEYS, prefix, 0)

    def place(slot, col, key):
        at = fill[key]
        edges[at] = slot * owners + lax.rem(col, owners)
        fill[key] = at + 1

    over_slots(place)


def spread_piece(piece, spread):
    value = piece[...]
    for chip in range(spread.shape[0]):
        spread[chip] = value


def solve_first(rows, owners, levels, held, own_inverse, their_inverse, piece, spread, buf, sems):
    inverses = (own_inverse, their_inverse)
    picks = [find_row(levels, owners, member, rows, 0) for member in range(MEMBERS)]

    def copy(member):
        return pltpu.make_async_copy(
            inverses[member].at[jnp.maximum(picks[member], 0)], buf.at[member], sems.at[member]
        )

    for member in range(MEMBERS):
        copy(member).start()
    for member in range(MEMBERS):
        at = slot_of(member)
        copy(member).wait()
        row = held[member * rows + jnp.maximum(picks[member], 0)].astype(jnp.bfloat16)
        solved = times_transposed(row, buf[member])
        piece[at] = jnp.where(picks[member] >= 0, solved, 0.0).astype(jnp.bfloat16)
    spread_piece(piece, spread)


def prepare_level(level, rows, width_k, owners, levels, edges, starts, held_in, *refs):
    if level:
        store, *refs = refs
    tiles, inverses = refs[:MEMBERS], refs[MEMBERS : 2 * MEMBERS]
    held, totals, ready, info, buf, blocks, sems, block_sems, ready_sems = refs[2 * MEMBERS :]
    slots = 1 + READY
    picks = [find_row(levels, owners, member, rows, level + 1) for member in range(MEMBERS)]

    def tile_of(member, i):
        code = edges[i] // owners - member * rows * width_k
        return tiles[member].at[code // width_k, lax.rem(code, width_k)]

    def ready_copy(member, place, source):
        return pltpu.make_async_copy(
            source, ready.at[member, place], ready_sems.at[member * slots + place]
        )

    def late_copy(member, first, i):
        at = lax.rem(i, RING)
        return pltpu.make_async_copy(tile_of(member, first + i), buf.at[at], sems.at[at])

    def block_copy(first, i):
        at = lax.rem(i, RING)
        place = lax.rem(edges[first + i], owners)
        return pltpu.make_async_copy(store.at[level - 1, place], blocks.at[at], block_sems.at[at])

    late = []
    if level:
        for member in range(MEMBERS):
            key = bucket(level - 1, False, member)
            late.append((starts[key], starts[key + 1] - starts[key]))
        first, many = late[0]

        def begin(i, unused, first=first):
            late_copy(0, first, i).start()
            block_copy(first, i).start()
            return unused

        lax.fori_loop(0, jnp.minimum(many, RING), begin, 0)

    urgent = []
    for member in range(MEMBERS):
        key = bucket(level, True, member)
        first, many = starts[key], starts[key + 1] - starts[key]
        urgent.append(jnp.minimum(many, READY))
        info[member] = jnp.where(picks[member] >= 0, many, 0)
        ready_copy(member, 0, inverses[member].at[jnp.maximum(picks[member], 0)]).start()

        def fetch(i, unused, member=member, first=first):
            ready_copy(member, 1 + i, tile_of(member, first + i)).start()
            return unused

        lax.fori_loop(0, urgent[member], fetch, 0)

    held[...] = held_in[...]
    if level:
        for member in range(MEMBERS):
            first, many = late[member]
            if member:

                def begin(i, unused, member=member, first=first):
                    late_copy(member, first, i).start()
                    block_copy(first, i).start()
                    return unused

                lax.fori_loop(0, jnp.minimum(many, RING), begin, 0)

            def absorb(i, unused, member=member, first=first, many=many):
                late_copy(member, first, i).wait()
                block_copy(first, i).wait()
                row = edges[first + i] // (owners * width_k)
                at = lax.rem(i, RING)
                given = times_transposed(blocks[at], buf[at])
                held[row] = held[row] - given

                @pl.when(i + RING < many)
                def _():
                    late_copy(member, first, i + RING).start()
                    block_copy(first, i + RING).start()

                return unused

            lax.fori_loop(0, many, absorb, 0)

    for member in range(MEMBERS):
        totals[member] = held[member * rows + jnp.maximum(picks[member], 0)]
        ready_copy(member, 0, inverses[member].at[0]).wait()

        def settle(i, unused, member=member):
            ready_copy(member, 1 + i, tiles[member].at[0, 0]).wait()
            return unused

        lax.fori_loop(0, urgent[member], settle, 0)


def solve_level(level, width_k, owners, edges, starts, info, totals, ready, received, *refs):
    tiles, refs = refs[:MEMBERS], refs[MEMBERS:]
    last = level == LEVELS - 1
    if last:
        piece, buf, sems = refs
    else:
        piece, spread, store, buf, sems, keep_sem = refs[1 if level > 1 else 0 :]
        keep = pltpu.make_async_copy(received, store.at[level - 1], keep_sem.at[0])
        keep.start()
    extra = width_k - READY

    def extra_copy(member, i):
        code = edges[starts[bucket(level - 1, True, member)] + i] // owners
        code = code - member * tiles[member].shape[0] * width_k
        at = member * extra + i - READY
        return pltpu.make_async_copy(
            tiles[member].at[code // width_k, lax.rem(code, width_k)], buf.at[at], sems.at[at]
        )

    for member in range(MEMBERS):

        def begin(i, unused, member=member):
            extra_copy(member, i).start()
            return unused

        lax.fori_loop(READY, info[member], begin, 0)

    for member in range(MEMBERS):
        at = slot_of(member)
        many = info[member]

        @pl.when(many == 0)
        def _(at=at):
            piece[at] = jnp.zeros(piece.shape[1:], piece.dtype)

        @pl.when(many > 0)
        def _(member=member, at=at, many=many):
            first = starts[bucket(level - 1, True, member)]
            near = jnp.minimum(many, READY)

            def absorb(group, total):
                for u in range(GROUP):
                    i = group * GROUP + u
                    here = jnp.minimum(i, near - 1)
                    block = received[lax.rem(edges[first + here], owners)]
                    block = jnp.where(i < near, block, jnp.zeros_like(block))
                    total = total - times_transposed(block, ready[member, 1 + here])
                return total

            def absorb_extra(i, total):
                extra_copy(member, i).wait()
                block = received[lax.rem(edges[first + i], owners)]
                return total - times_transposed(block, buf[member * extra + i - READY])

            total = lax.fori_loop(0, (near + GROUP - 1) // GROUP, absorb, totals[member])
            total = lax.fori_loop(READY, many, absorb_extra, total)
            solved = times_transposed(total.astype(jnp.bfloat16), ready[member, 0])
            piece[at] = solved.astype(jnp.bfloat16)

    if not last:
        spread_piece(piece, spread)
        keep.wait()


def collect_rows(rows, owners, base, levels, *refs):
    pieces, outs = refs[:-MEMBERS], refs[-MEMBERS:]
    if base:
        befores, pieces = pieces[:MEMBERS], pieces[MEMBERS:]
    for member in range(MEMBERS):
        if base:
            outs[member][...] = befores[member][...]
        for i, piece in enumerate(pieces):
            row = find_row(levels, owners, member, rows, base + i)

            @pl.when(row >= 0)
            def _(piece=piece, member=member, row=row):
                outs[member][row] = piece[slot_of(member)]


def local(right_sides, lower_tiles, diag_inverse, tile_columns, tile_counts, level_sets):
    owners = lax.axis_size(ROWS)
    chips = lax.axis_size(CHIPS)
    core = lax.axis_index(CORE)
    rows, unused_one, width_k = tile_columns.shape
    part = right_sides.shape[3] // MEMBERS
    lanes = right_sides.shape[2]
    block = (part, lanes)
    tile = lower_tiles.shape[3:]

    def swapped(value):
        return lax.ppermute(value, CORE, SWAP)

    levels = level_sets.reshape(-1)
    rhs = jnp.swapaxes(right_sides[:, 0], 1, 2)
    rhs_mine = lax.dynamic_slice_in_dim(rhs, core * part, part, 1)
    rhs_theirs = swapped(lax.dynamic_slice_in_dim(rhs, (1 - core) * part, part, 1))
    held = jnp.concatenate([rhs_mine, rhs_theirs])
    inverses = (diag_inverse[:, 0], swapped(diag_inverse[:, 0]))

    def call(kernel, name, out_shape, out_specs, in_specs, scratch, operands, flops, moved):
        return pl.pallas_call(
            kernel,
            out_shape=out_shape,
            in_specs=in_specs,
            out_specs=out_specs,
            scratch_shapes=scratch,
            compiler_params=pltpu.CompilerParams(vmem_limit_bytes=GRANT),
            cost_estimate=pl.CostEstimate(flops=flops, bytes_accessed=moved, transcendentals=0),
            name=name,
        )(*operands)

    piece_shape = jax.ShapeDtypeStruct((MEMBERS, *block), jnp.bfloat16)
    spread_shape = jax.ShapeDtypeStruct((chips, MEMBERS, *block), jnp.bfloat16)

    store_shape = jax.ShapeDtypeStruct((LEVELS - 2, owners, *block), jnp.bfloat16)

    def exchanged(spread):
        return lax.all_to_all(spread, CHIPS, 0, 0, tiled=True).reshape(owners, *block)

    piece, spread = call(
        functools.partial(solve_first, rows, owners),
        "solve_0",
        (piece_shape, spread_shape),
        (vmem(), vmem()),
        [smem(), vmem(), anywhere(), anywhere()],
        [pltpu.VMEM((MEMBERS, *tile), jnp.bfloat16), pltpu.SemaphoreType.DMA((MEMBERS,))],
        (levels, held, *inverses),
        4 << 20,
        1 << 18,
    )
    pieces = [piece]
    arriving = exchanged(spread)

    own_tiles, columns_own, counts_own, unused_tie = lax.optimization_barrier(
        (lower_tiles[:, 0], tile_columns[:, 0], tile_counts[:, 0], piece)
    )
    tiles = (own_tiles, swapped(own_tiles))
    columns = jnp.concatenate([columns_own, swapped(columns_own)]).reshape(-1)
    counts = jnp.concatenate([counts_own, swapped(counts_own)])
    edges, starts = call(
        functools.partial(list_edges, owners),
        "list_edges",
        (
            jax.ShapeDtypeStruct((columns.size,), jnp.int32),
            jax.ShapeDtypeStruct((KEYS + 1,), jnp.int32),
        ),
        (smem(), smem()),
        [smem()] * 3,
        [pltpu.SMEM((KEYS,), jnp.int32)],
        (columns, counts, levels),
        8 << 20,
        1 << 20,
    )

    def prepare(level, store, held):
        return call(
            functools.partial(prepare_level, level, rows, width_k, owners),
            f"prepare_{level}",
            (
                jax.ShapeDtypeStruct(held.shape, held.dtype),
                jax.ShapeDtypeStruct((MEMBERS, *block), jnp.float32),
                jax.ShapeDtypeStruct((MEMBERS, 1 + READY, *tile), jnp.bfloat16),
                jax.ShapeDtypeStruct((MEMBERS,), jnp.int32),
            ),
            (vmem(), vmem(), vmem(), smem()),
            [smem()] * 3 + [vmem()] + [anywhere()] * (2 * MEMBERS + (1 if level else 0)),
            [
                pltpu.VMEM((RING, *tile), jnp.bfloat16),
                pltpu.VMEM((RING, *block), jnp.bfloat16),
                pltpu.SemaphoreType.DMA((RING,)),
                pltpu.SemaphoreType.DMA((RING,)),
                pltpu.SemaphoreType.DMA((MEMBERS * (1 + READY),)),
            ],
            (levels, edges, starts, held, *((store,) if level else ()), *tiles, *inverses),
            32 << 20,
            1 << 20,
        )

    def solve(level, received, store, totals, ready, info):
        last = level == LEVELS - 1
        held_store = (store,) if 1 < level and not last else ()
        operands = (edges, starts, info, totals, ready, received, *tiles, *held_store)
        extra = MEMBERS * (width_k - READY)
        return pl.pallas_call(
            functools.partial(solve_level, level, width_k, owners),
            out_shape=(piece_shape,) if last else (piece_shape, spread_shape, store_shape),
            in_specs=[smem()] * 3 + [vmem()] * 3 + [anywhere()] * (MEMBERS + len(held_store)),
            out_specs=(vmem(),) if last else (vmem(), vmem(), anywhere()),
            scratch_shapes=[
                pltpu.VMEM((extra, *tile), jnp.bfloat16),
                pltpu.SemaphoreType.DMA((extra,)),
            ]
            + ([] if last else [pltpu.SemaphoreType.DMA((1,))]),
            input_output_aliases={len(operands) - 1: 2} if held_store else {},
            compiler_params=pltpu.CompilerParams(vmem_limit_bytes=GRANT),
            cost_estimate=pl.CostEstimate(
                flops=4 << 20, bytes_accessed=1 << 18, transcendentals=0
            ),
            name=f"solve_{level}",
        )(*operands)

    def collect(base, befores, pieces):
        return call(
            functools.partial(collect_rows, rows, owners, base),
            "collect_rows",
            (jax.ShapeDtypeStruct((rows, *block), jnp.bfloat16),) * MEMBERS,
            (vmem(),) * MEMBERS,
            [smem()] + [vmem()] * (len(befores) + len(pieces)),
            [],
            (levels, *befores, *pieces),
            1 << 10,
            1 << 18,
        )

    store = None
    for level in range(1, LEVELS):
        held, totals, ready, info = prepare(level - 1, store, held)
        if level == LEVELS - 1:
            early = collect(0, (), pieces)
        piece, *more = solve(level, arriving, store, totals, ready, info)
        if more:
            spread, store = more
            pieces.append(piece)
            arriving = exchanged(spread)

    mine, theirs = collect(LEVELS - 1, early, (piece,))
    theirs = swapped(theirs)
    both = jnp.concatenate([mine, theirs], 1)
    crossed = jnp.concatenate([theirs, mine], 1)
    return jnp.swapaxes(jnp.where(core == 0, both, crossed), 1, 2)[:, None]


def solution(mesh):
    finer = Mesh(mesh.devices.reshape(4, 4, 4, 2), ROWS)
    return jax.shard_map(
        local,
        mesh=finer,
        in_specs=(
            P(None, ROWS, None, None),
            P(None, ROWS, None, None, None),
            P(None, ROWS, None, None),
            P(None, ROWS, None),
            P(None, ROWS),
            P(),
        ),
        out_specs=P(None, ROWS, None, None),
        check_vma=False,
    )
```

```python
import functools

import jax
import jax.numpy as jnp
from jax import lax
from jax.experimental import pallas as pl
from jax.experimental.pallas import tpu as pltpu
from jax.sharding import Mesh
from jax.sharding import PartitionSpec as P

LEVELS = 16
ROWS = ("rows_0", "rows_1", "rows_2", "rows_3")
CHIPS = ("rows_2", "rows_0", "rows_1")
CORE = "rows_3"
SWAP = ((0, 1), (1, 0))
MEMBERS = 2
KEYS = LEVELS * 2 * MEMBERS
RING = 8
GROUP = 3
READY = 3
GRANT = 50 << 20


def smem():
    return pl.BlockSpec(memory_space=pltpu.SMEM)


def vmem():
    return pl.BlockSpec(memory_space=pltpu.VMEM)


def anywhere():
    return pl.BlockSpec(memory_space=pltpu.HBM)


def bucket(level, urgent, member):
    return (level * 2 + (0 if urgent else 1)) * MEMBERS + member


def times_transposed(rows, tile):
    return lax.dot_general(
        rows, tile, (((1,), (1,)), ((), ())), preferred_element_type=jnp.float32
    )


def device_of(member, owners_index):
    core = lax.axis_index(CORE)
    return owners_index + (1 - 2 * core) * member


def slot_of(member):
    core = lax.axis_index(CORE)
    return core if member == 0 else 1 - core


def find_row(levels, owners, member, rows, level):
    own = device_of(member, lax.axis_index(ROWS))
    pick = jnp.int32(-1)
    for s in range(rows):
        pick = jnp.where(levels[s * owners + own] == level, s, pick)
    return pick


def list_edges(owners, line, columns, counts, levels, edges, starts, fill):
    rows = counts.shape[0] // MEMBERS
    width_k = columns.shape[0] // counts.shape[0]

    def clear(key, unused):
        fill[key] = 0
        return unused

    lax.fori_loop(0, KEYS, clear, 0)

    def over_slots(visit):
        for member in range(MEMBERS):
            own = device_of(member, lax.axis_index(ROWS))

            def each_row(row, unused, member=member, own=own):
                next_level = levels[row * owners + own]
                at = member * rows + row

                def each_slot(slot, unused):
                    col = columns[at * width_k + slot]
                    level = levels[col]
                    late = jnp.where(next_level == level + 1, 0, 1)
                    visit(at * width_k + slot, col, (level * 2 + late) * MEMBERS + member)
                    return unused

                return lax.fori_loop(0, counts[at], each_slot, unused)

            lax.fori_loop(0, rows, each_row, 0)

    def count(slot, col, key):
        fill[key] = fill[key] + 1

    over_slots(count)

    def prefix(key, total):
        starts[key] = total
        here = fill[key]
        fill[key] = total
        return total + here

    starts[KEYS] = lax.fori_loop(0, KEYS, prefix, 0)

    def place(slot, col, key):
        at = fill[key]
        chip = lax.rem(col, owners) // MEMBERS
        turned = lax.rem(chip, line) * (owners // MEMBERS // line) + chip // line
        edges[at] = slot * owners + turned * MEMBERS + lax.rem(col, MEMBERS)
        fill[key] = at + 1

    over_slots(place)


def spread_piece(piece, spread):
    value = piece[...]
    for chip in range(spread.shape[0]):
        spread[chip] = value


def solve_first(rows, owners, levels, held, own_inverse, their_inverse, piece, spread, buf, sems):
    inverses = (own_inverse, their_inverse)
    picks = [find_row(levels, owners, member, rows, 0) for member in range(MEMBERS)]

    def copy(member):
        return pltpu.make_async_copy(
            inverses[member].at[jnp.maximum(picks[member], 0)], buf.at[member], sems.at[member]
        )

    for member in range(MEMBERS):
        copy(member).start()
    for member in range(MEMBERS):
        at = slot_of(member)
        copy(member).wait()
        row = held[member * rows + jnp.maximum(picks[member], 0)].astype(jnp.bfloat16)
        solved = times_transposed(row, buf[member])
        piece[at] = jnp.where(picks[member] >= 0, solved, 0.0).astype(jnp.bfloat16)
    spread_piece(piece, spread)


def prepare_level(level, rows, width_k, owners, levels, edges, starts, held_in, *refs):
    if level:
        received, *refs = refs
    tiles, inverses = refs[:MEMBERS], refs[MEMBERS : 2 * MEMBERS]
    held, totals, ready, info, buf, sems, ready_sems = refs[2 * MEMBERS :]
    slots = 1 + READY
    picks = [find_row(levels, owners, member, rows, level + 1) for member in range(MEMBERS)]

    def tile_of(member, i):
        code = edges[i] // owners - member * rows * width_k
        return tiles[member].at[code // width_k, lax.rem(code, width_k)]

    def ready_copy(member, place, source):
        return pltpu.make_async_copy(
            source, ready.at[member, place], ready_sems.at[member * slots + place]
        )

    def late_copy(member, first, i):
        at = lax.rem(i, RING)
        return pltpu.make_async_copy(tile_of(member, first + i), buf.at[at], sems.at[at])

    late = []
    if level:
        for member in range(MEMBERS):
            key = bucket(level - 1, False, member)
            late.append((starts[key], starts[key + 1] - starts[key]))
        first, many = late[0]

        def begin(i, unused, first=first):
            late_copy(0, first, i).start()
            return unused

        lax.fori_loop(0, jnp.minimum(many, RING), begin, 0)

    urgent = []
    for member in range(MEMBERS):
        key = bucket(level, True, member)
        first, many = starts[key], starts[key + 1] - starts[key]
        urgent.append(jnp.minimum(many, READY))
        info[member] = jnp.where(picks[member] >= 0, many, 0)
        ready_copy(member, 0, inverses[member].at[jnp.maximum(picks[member], 0)]).start()

        def fetch(i, unused, member=member, first=first):
            ready_copy(member, 1 + i, tile_of(member, first + i)).start()
            return unused

        lax.fori_loop(0, urgent[member], fetch, 0)

    held[...] = held_in[...]
    if level:
        for member in range(MEMBERS):
            first, many = late[member]
            if member:

                def begin(i, unused, member=member, first=first):
                    late_copy(member, first, i).start()
                    return unused

                lax.fori_loop(0, jnp.minimum(many, RING), begin, 0)

            def absorb(i, unused, member=member, first=first, many=many):
                late_copy(member, first, i).wait()
                code = edges[first + i]
                row = code // (owners * width_k)
                given = times_transposed(received[lax.rem(code, owners)], buf[lax.rem(i, RING)])
                held[row] = held[row] - given

                @pl.when(i + RING < many)
                def _():
                    late_copy(member, first, i + RING).start()

                return unused

            lax.fori_loop(0, many, absorb, 0)

    for member in range(MEMBERS):
        totals[member] = held[member * rows + jnp.maximum(picks[member], 0)]
        ready_copy(member, 0, inverses[member].at[0]).wait()

        def settle(i, unused, member=member):
            ready_copy(member, 1 + i, tiles[member].at[0, 0]).wait()
            return unused

        lax.fori_loop(0, urgent[member], settle, 0)


def solve_level(level, width_k, owners, edges, starts, info, totals, ready, received, *refs):
    tiles, (piece, *spread, buf, sems) = refs[:MEMBERS], refs[MEMBERS:]
    extra = width_k - READY

    def extra_copy(member, i):
        code = edges[starts[bucket(level - 1, True, member)] + i] // owners
        code = code - member * tiles[member].shape[0] * width_k
        at = member * extra + i - READY
        return pltpu.make_async_copy(
            tiles[member].at[code // width_k, lax.rem(code, width_k)], buf.at[at], sems.at[at]
        )

    for member in range(MEMBERS):

        def begin(i, unused, member=member):
            extra_copy(member, i).start()
            return unused

        lax.fori_loop(READY, info[member], begin, 0)

    for member in range(MEMBERS):
        at = slot_of(member)
        many = info[member]

        @pl.when(many == 0)
        def _(at=at):
            piece[at] = jnp.zeros(piece.shape[1:], piece.dtype)

        @pl.when(many > 0)
        def _(member=member, at=at, many=many):
            first = starts[bucket(level - 1, True, member)]
            near = jnp.minimum(many, READY)

            def absorb(group, total):
                for u in range(GROUP):
                    i = group * GROUP + u
                    here = jnp.minimum(i, near - 1)
                    block = received[lax.rem(edges[first + here], owners)]
                    block = jnp.where(i < near, block, jnp.zeros_like(block))
                    total = total - times_transposed(block, ready[member, 1 + here])
                return total

            def absorb_extra(i, total):
                extra_copy(member, i).wait()
                block = received[lax.rem(edges[first + i], owners)]
                return total - times_transposed(block, buf[member * extra + i - READY])

            total = lax.fori_loop(0, (near + GROUP - 1) // GROUP, absorb, totals[member])
            total = lax.fori_loop(READY, many, absorb_extra, total)
            solved = times_transposed(total.astype(jnp.bfloat16), ready[member, 0])
            piece[at] = solved.astype(jnp.bfloat16)

    if spread:
        spread_piece(piece, *spread)


def collect_rows(rows, owners, base, levels, *refs):
    pieces, outs = refs[:-MEMBERS], refs[-MEMBERS:]
    if base:
        befores, pieces = pieces[:MEMBERS], pieces[MEMBERS:]
    for member in range(MEMBERS):
        if base:
            outs[member][...] = befores[member][...]
        for i, piece in enumerate(pieces):
            row = find_row(levels, owners, member, rows, base + i)

            @pl.when(row >= 0)
            def _(piece=piece, member=member, row=row):
                outs[member][row] = piece[slot_of(member)]


def local(right_sides, lower_tiles, diag_inverse, tile_columns, tile_counts, level_sets):
    owners = lax.axis_size(ROWS)
    chips = lax.axis_size(CHIPS)
    core = lax.axis_index(CORE)
    rows, unused_one, width_k = tile_columns.shape
    part = right_sides.shape[3] // MEMBERS
    lanes = right_sides.shape[2]
    block = (part, lanes)
    tile = lower_tiles.shape[3:]

    def swapped(value):
        return lax.ppermute(value, CORE, SWAP)

    levels = level_sets.reshape(-1)
    rhs = jnp.swapaxes(right_sides[:, 0], 1, 2)
    rhs_mine = lax.dynamic_slice_in_dim(rhs, core * part, part, 1)
    rhs_theirs = swapped(lax.dynamic_slice_in_dim(rhs, (1 - core) * part, part, 1))
    held = jnp.concatenate([rhs_mine, rhs_theirs])
    inverses = (diag_inverse[:, 0], swapped(diag_inverse[:, 0]))

    def call(kernel, name, out_shape, out_specs, in_specs, scratch, operands, flops, moved):
        return pl.pallas_call(
            kernel,
            out_shape=out_shape,
            in_specs=in_specs,
            out_specs=out_specs,
            scratch_shapes=scratch,
            compiler_params=pltpu.CompilerParams(vmem_limit_bytes=GRANT),
            cost_estimate=pl.CostEstimate(flops=flops, bytes_accessed=moved, transcendentals=0),
            name=name,
        )(*operands)

    piece_shape = jax.ShapeDtypeStruct((MEMBERS, *block), jnp.bfloat16)
    spread_shape = jax.ShapeDtypeStruct((chips, MEMBERS, *block), jnp.bfloat16)

    def exchanged(spread):
        return lax.all_to_all(spread, CHIPS, 0, 0, tiled=True).reshape(owners, *block)

    piece, spread = call(
        functools.partial(solve_first, rows, owners),
        "solve_0",
        (piece_shape, spread_shape),
        (vmem(), vmem()),
        [smem(), vmem(), anywhere(), anywhere()],
        [pltpu.VMEM((MEMBERS, *tile), jnp.bfloat16), pltpu.SemaphoreType.DMA((MEMBERS,))],
        (levels, held, *inverses),
        4 << 20,
        1 << 18,
    )
    pieces = [piece]
    arriving = exchanged(spread)

    own_tiles, columns_own, counts_own, unused_tie = lax.optimization_barrier(
        (lower_tiles[:, 0], tile_columns[:, 0], tile_counts[:, 0], piece)
    )
    tiles = (own_tiles, swapped(own_tiles))
    columns = jnp.concatenate([columns_own, swapped(columns_own)]).reshape(-1)
    counts = jnp.concatenate([counts_own, swapped(counts_own)])
    edges, starts = call(
        functools.partial(list_edges, owners, lax.axis_size(CHIPS[0])),
        "list_edges",
        (
            jax.ShapeDtypeStruct((columns.size,), jnp.int32),
            jax.ShapeDtypeStruct((KEYS + 1,), jnp.int32),
        ),
        (smem(), smem()),
        [smem()] * 3,
        [pltpu.SMEM((KEYS,), jnp.int32)],
        (columns, counts, levels),
        8 << 20,
        1 << 20,
    )

    def prepare(level, received, held):
        return call(
            functools.partial(prepare_level, level, rows, width_k, owners),
            f"prepare_{level}",
            (
                jax.ShapeDtypeStruct(held.shape, held.dtype),
                jax.ShapeDtypeStruct((MEMBERS, *block), jnp.float32),
                jax.ShapeDtypeStruct((MEMBERS, 1 + READY, *tile), jnp.bfloat16),
                jax.ShapeDtypeStruct((MEMBERS,), jnp.int32),
            ),
            (vmem(), vmem(), vmem(), smem()),
            [smem()] * 3 + [vmem()] * (2 if level else 1) + [anywhere()] * (2 * MEMBERS),
            [
                pltpu.VMEM((RING, *tile), jnp.bfloat16),
                pltpu.SemaphoreType.DMA((RING,)),
                pltpu.SemaphoreType.DMA((MEMBERS * (1 + READY),)),
            ],
            (levels, edges, starts, held, *((received,) if level else ()), *tiles, *inverses),
            32 << 20,
            1 << 20,
        )

    def solve(level, received, totals, ready, info):
        last = level == LEVELS - 1
        return call(
            functools.partial(solve_level, level, width_k, owners),
            f"solve_{level}",
            (piece_shape,) if last else (piece_shape, spread_shape),
            (vmem(),) if last else (vmem(), vmem()),
            [smem()] * 3 + [vmem()] * 3 + [anywhere()] * MEMBERS,
            [
                pltpu.VMEM((MEMBERS * (width_k - READY), *tile), jnp.bfloat16),
                pltpu.SemaphoreType.DMA((MEMBERS * (width_k - READY),)),
            ],
            (edges, starts, info, totals, ready, received, *tiles),
            4 << 20,
            1 << 18,
        )

    def collect(base, befores, pieces):
        return call(
            functools.partial(collect_rows, rows, owners, base),
            "collect_rows",
            (jax.ShapeDtypeStruct((rows, *block), jnp.bfloat16),) * MEMBERS,
            (vmem(),) * MEMBERS,
            [smem()] + [vmem()] * (len(befores) + len(pieces)),
            [],
            (levels, *befores, *pieces),
            1 << 10,
            1 << 18,
        )

    received = None
    for level in range(1, LEVELS):
        held, totals, ready, info = prepare(level - 1, received, held)
        if level == LEVELS - 1:
            early = collect(0, (), pieces)
        received = arriving
        piece, *spread = solve(level, received, totals, ready, info)
        if level < LEVELS - 1:
            pieces.append(piece)
            arriving = exchanged(*spread)

    mine, theirs = collect(LEVELS - 1, early, (piece,))
    theirs = swapped(theirs)
    both = jnp.concatenate([mine, theirs], 1)
    crossed = jnp.concatenate([theirs, mine], 1)
    return jnp.swapaxes(jnp.where(core == 0, both, crossed), 1, 2)[:, None]


def solution(mesh):
    finer = Mesh(mesh.devices.reshape(4, 4, 4, 2), ROWS)
    return jax.shard_map(
        local,
        mesh=finer,
        in_specs=(
            P(None, ROWS, None, None),
            P(None, ROWS, None, None, None),
            P(None, ROWS, None, None),
            P(None, ROWS, None),
            P(None, ROWS),
            P(),
        ),
        out_specs=P(None, ROWS, None, None),
        check_vma=False,
    )
```

```python
import functools

import jax
import jax.numpy as jnp
from jax import lax
from jax.experimental import pallas as pl
from jax.experimental.pallas import tpu as pltpu
from jax.sharding import Mesh
from jax.sharding import PartitionSpec as P

LEVELS = 16
ROWS = ("rows_0", "rows_1", "rows_2", "rows_3")
CHIPS = ("rows_0", "rows_1", "rows_2")
CORE = "rows_3"
SWAP = ((0, 1), (1, 0))
MEMBERS = 2
KEYS = LEVELS * 2 * MEMBERS
RING = 8
FAN = 8
GROUP = 3
READY = 6
GRANT = 50 << 20


def smem():
    return pl.BlockSpec(memory_space=pltpu.SMEM)


def vmem():
    return pl.BlockSpec(memory_space=pltpu.VMEM)


def anywhere():
    return pl.BlockSpec(memory_space=pltpu.HBM)


def bucket(level, urgent, member):
    return (level * 2 + (0 if urgent else 1)) * MEMBERS + member


def times_transposed(rows, tile):
    return lax.dot_general(
        rows, tile, (((1,), (1,)), ((), ())), preferred_element_type=jnp.float32
    )


def device_of(member, owners_index):
    core = lax.axis_index(CORE)
    return owners_index + (1 - 2 * core) * member


def slot_of(member):
    core = lax.axis_index(CORE)
    return core if member == 0 else 1 - core


def find_row(levels, owners, member, rows, level):
    own = device_of(member, lax.axis_index(ROWS))
    pick = jnp.int32(-1)
    for s in range(rows):
        pick = jnp.where(levels[s * owners + own] == level, s, pick)
    return pick


def list_edges(owners, columns, counts, levels, edges, starts, fill):
    rows = counts.shape[0] // MEMBERS
    width_k = columns.shape[0] // counts.shape[0]

    def clear(key, unused):
        fill[key] = 0
        return unused

    lax.fori_loop(0, KEYS, clear, 0)

    def over_slots(visit):
        for member in range(MEMBERS):
            own = device_of(member, lax.axis_index(ROWS))

            def each_row(row, unused, member=member, own=own):
                next_level = levels[row * owners + own]
                at = member * rows + row

                def each_slot(slot, unused):
                    col = columns[at * width_k + slot]
                    level = levels[col]
                    late = jnp.where(next_level == level + 1, 0, 1)
                    visit(at * width_k + slot, col, (level * 2 + late) * MEMBERS + member)
                    return unused

                return lax.fori_loop(0, counts[at], each_slot, unused)

            lax.fori_loop(0, rows, each_row, 0)

    def count(slot, col, key):
        fill[key] = fill[key] + 1

    over_slots(count)

    def prefix(key, total):
        starts[key] = total
        here = fill[key]
        fill[key] = total
        return total + here

    starts[KEYS] = lax.fori_loop(0, KEYS, prefix, 0)

    def place(slot, col, key):
        at = fill[key]
        edges[at] = slot * owners + lax.rem(col, owners)
        fill[key] = at + 1

    over_slots(place)


def spread_slot(member, piece, spread, fan, sems):
    at = slot_of(member)
    value = piece[at]
    for i in range(FAN):
        fan[member, i] = value
    copies = [
        pltpu.make_async_copy(
            fan.at[member], spread.at[pl.ds(i * FAN, FAN), at], sems.at[member, i]
        )
        for i in range(spread.shape[0] // FAN)
    ]
    for copy in copies:
        copy.start()
    return copies


def solve_first(rows, owners, levels, held, own_inverse, their_inverse, piece, spread, buf, sems, fan, fan_sems):
    inverses = (own_inverse, their_inverse)
    picks = [find_row(levels, owners, member, rows, 0) for member in range(MEMBERS)]

    def copy(member):
        return pltpu.make_async_copy(
            inverses[member].at[jnp.maximum(picks[member], 0)], buf.at[member], sems.at[member]
        )

    copies = []
    for member in range(MEMBERS):
        copy(member).start()
    for member in range(MEMBERS):
        at = slot_of(member)
        copy(member).wait()
        row = held[member * rows + jnp.maximum(picks[member], 0)].astype(jnp.bfloat16)
        solved = times_transposed(row, buf[member])
        piece[at] = jnp.where(picks[member] >= 0, solved, 0.0).astype(jnp.bfloat16)
        copies += spread_slot(member, piece, spread, fan, fan_sems)
    for spreading in copies:
        spreading.wait()


def prepare_level(level, rows, width_k, owners, levels, edges, starts, held_in, *refs):
    if level:
        store, *refs = refs
    tiles, inverses = refs[:MEMBERS], refs[MEMBERS : 2 * MEMBERS]
    held, totals, ready, info, buf, blocks, sems, block_sems, ready_sems = refs[2 * MEMBERS :]
    slots = 1 + READY
    picks = [find_row(levels, owners, member, rows, level + 1) for member in range(MEMBERS)]

    def tile_of(member, i):
        code = edges[i] // owners - member * rows * width_k
        return tiles[member].at[code // width_k, lax.rem(code, width_k)]

    def ready_copy(member, place, source):
        return pltpu.make_async_copy(
            source, ready.at[member, place], ready_sems.at[member * slots + place]
        )

    def late_copy(member, first, i):
        at = lax.rem(i, RING)
        return pltpu.make_async_copy(tile_of(member, first + i), buf.at[at], sems.at[at])

    def block_copy(first, i):
        at = lax.rem(i, RING)
        place = lax.rem(edges[first + i], owners)
        return pltpu.make_async_copy(store.at[level - 1, place], blocks.at[at], block_sems.at[at])

    late = []
    if level:
        for member in range(MEMBERS):
            key = bucket(level - 1, False, member)
            late.append((starts[key], starts[key + 1] - starts[key]))
        first, many = late[0]

        def begin(i, unused, first=first):
            late_copy(0, first, i).start()
            block_copy(first, i).start()
            return unused

        lax.fori_loop(0, jnp.minimum(many, RING), begin, 0)

    urgent = []
    for member in range(MEMBERS):
        key = bucket(level, True, member)
        first, many = starts[key], starts[key + 1] - starts[key]
        urgent.append(jnp.minimum(many, READY))
        info[member] = jnp.where(picks[member] >= 0, many, 0)
        ready_copy(member, 0, inverses[member].at[jnp.maximum(picks[member], 0)]).start()

        def fetch(i, unused, member=member, first=first):
            ready_copy(member, 1 + i, tile_of(member, first + i)).start()
            return unused

        lax.fori_loop(0, urgent[member], fetch, 0)

    held[...] = held_in[...]
    if level:
        for member in range(MEMBERS):
            first, many = late[member]
            if member:

                def begin(i, unused, member=member, first=first):
                    late_copy(member, first, i).start()
                    block_copy(first, i).start()
                    return unused

                lax.fori_loop(0, jnp.minimum(many, RING), begin, 0)

            def absorb(i, unused, member=member, first=first, many=many):
                late_copy(member, first, i).wait()
                block_copy(first, i).wait()
                row = edges[first + i] // (owners * width_k)
                at = lax.rem(i, RING)
                given = times_transposed(blocks[at], buf[at])
                held[row] = held[row] - given

                @pl.when(i + RING < many)
                def _():
                    late_copy(member, first, i + RING).start()
                    block_copy(first, i + RING).start()

                return unused

            lax.fori_loop(0, many, absorb, 0)

    for member in range(MEMBERS):
        totals[member] = held[member * rows + jnp.maximum(picks[member], 0)]
        ready_copy(member, 0, inverses[member].at[0]).wait()

        def settle(i, unused, member=member):
            ready_copy(member, 1 + i, tiles[member].at[0, 0]).wait()
            return unused

        lax.fori_loop(0, urgent[member], settle, 0)


def solve_level(level, width_k, owners, edges, starts, info, totals, ready, received, *refs):
    tiles, refs = refs[:MEMBERS], refs[MEMBERS:]
    last = level == LEVELS - 1
    if last:
        piece, buf, sems = refs
    else:
        piece, spread, store, buf, sems, keep_sem, *fan = refs[1 if level > 1 else 0 :]
        keep = pltpu.make_async_copy(received, store.at[level - 1], keep_sem.at[0])
        keep.start()
    copies = []
    extra = width_k - READY

    def extra_copy(member, i):
        code = edges[starts[bucket(level - 1, True, member)] + i] // owners
        code = code - member * tiles[member].shape[0] * width_k
        at = member * extra + i - READY
        return pltpu.make_async_copy(
            tiles[member].at[code // width_k, lax.rem(code, width_k)], buf.at[at], sems.at[at]
        )

    for member in range(MEMBERS):

        def begin(i, unused, member=member):
            extra_copy(member, i).start()
            return unused

        lax.fori_loop(READY, info[member], begin, 0)

    for member in range(MEMBERS):
        at = slot_of(member)
        many = info[member]

        @pl.when(many == 0)
        def _(at=at):
            piece[at] = jnp.zeros(piece.shape[1:], piece.dtype)

        @pl.when(many > 0)
        def _(member=member, at=at, many=many):
            first = starts[bucket(level - 1, True, member)]
            near = jnp.minimum(many, READY)

            def absorb(group, total):
                for u in range(GROUP):
                    i = group * GROUP + u
                    here = jnp.minimum(i, near - 1)
                    block = received[lax.rem(edges[first + here], owners)]
                    block = jnp.where(i < near, block, jnp.zeros_like(block))
                    total = total - times_transposed(block, ready[member, 1 + here])
                return total

            def absorb_extra(i, total):
                extra_copy(member, i).wait()
                block = received[lax.rem(edges[first + i], owners)]
                return total - times_transposed(block, buf[member * extra + i - READY])

            total = lax.fori_loop(0, (near + GROUP - 1) // GROUP, absorb, totals[member])
            total = lax.fori_loop(READY, many, absorb_extra, total)
            solved = times_transposed(total.astype(jnp.bfloat16), ready[member, 0])
            piece[at] = solved.astype(jnp.bfloat16)

        if not last:
            copies += spread_slot(member, piece, spread, *fan)

    if not last:
        keep.wait()
        for copy in copies:
            copy.wait()


def collect_rows(rows, owners, base, levels, *refs):
    pieces, outs = refs[:-MEMBERS], refs[-MEMBERS:]
    if base:
        befores, pieces = pieces[:MEMBERS], pieces[MEMBERS:]
    for member in range(MEMBERS):
        if base:
            outs[member][...] = befores[member][...]
        for i, piece in enumerate(pieces):
            row = find_row(levels, owners, member, rows, base + i)

            @pl.when(row >= 0)
            def _(piece=piece, member=member, row=row):
                outs[member][row] = piece[slot_of(member)]


def local(right_sides, lower_tiles, diag_inverse, tile_columns, tile_counts, level_sets):
    owners = lax.axis_size(ROWS)
    chips = lax.axis_size(CHIPS)
    core = lax.axis_index(CORE)
    rows, unused_one, width_k = tile_columns.shape
    part = right_sides.shape[3] // MEMBERS
    lanes = right_sides.shape[2]
    block = (part, lanes)
    tile = lower_tiles.shape[3:]

    def swapped(value):
        return lax.ppermute(value, CORE, SWAP)

    levels = level_sets.reshape(-1)
    rhs = jnp.swapaxes(right_sides[:, 0], 1, 2)
    rhs_mine = lax.dynamic_slice_in_dim(rhs, core * part, part, 1)
    rhs_theirs = swapped(lax.dynamic_slice_in_dim(rhs, (1 - core) * part, part, 1))
    held = jnp.concatenate([rhs_mine, rhs_theirs])
    inverses = (diag_inverse[:, 0], swapped(diag_inverse[:, 0]))

    def call(kernel, name, out_shape, out_specs, in_specs, scratch, operands, flops, moved):
        return pl.pallas_call(
            kernel,
            out_shape=out_shape,
            in_specs=in_specs,
            out_specs=out_specs,
            scratch_shapes=scratch,
            compiler_params=pltpu.CompilerParams(vmem_limit_bytes=GRANT),
            cost_estimate=pl.CostEstimate(flops=flops, bytes_accessed=moved, transcendentals=0),
            name=name,
        )(*operands)

    piece_shape = jax.ShapeDtypeStruct((MEMBERS, *block), jnp.bfloat16)
    spread_shape = jax.ShapeDtypeStruct((chips, MEMBERS, *block), jnp.bfloat16)

    store_shape = jax.ShapeDtypeStruct((LEVELS - 2, owners, *block), jnp.bfloat16)

    fan = [
        pltpu.VMEM((MEMBERS, FAN, *block), jnp.bfloat16),
        pltpu.SemaphoreType.DMA((MEMBERS, chips // FAN)),
    ]

    def exchanged(spread):
        return lax.all_to_all(spread, CHIPS, 0, 0, tiled=True).reshape(owners, *block)

    piece, spread = call(
        functools.partial(solve_first, rows, owners),
        "solve_0",
        (piece_shape, spread_shape),
        (vmem(), anywhere()),
        [smem(), vmem(), anywhere(), anywhere()],
        [pltpu.VMEM((MEMBERS, *tile), jnp.bfloat16), pltpu.SemaphoreType.DMA((MEMBERS,)), *fan],
        (levels, held, *inverses),
        4 << 20,
        1 << 18,
    )
    pieces = [piece]
    arriving = exchanged(spread)

    own_tiles, columns_own, counts_own, unused_tie = lax.optimization_barrier(
        (lower_tiles[:, 0], tile_columns[:, 0], tile_counts[:, 0], piece)
    )
    tiles = (own_tiles, swapped(own_tiles))
    columns = jnp.concatenate([columns_own, swapped(columns_own)]).reshape(-1)
    counts = jnp.concatenate([counts_own, swapped(counts_own)])
    edges, starts = call(
        functools.partial(list_edges, owners),
        "list_edges",
        (
            jax.ShapeDtypeStruct((columns.size,), jnp.int32),
            jax.ShapeDtypeStruct((KEYS + 1,), jnp.int32),
        ),
        (smem(), smem()),
        [smem()] * 3,
        [pltpu.SMEM((KEYS,), jnp.int32)],
        (columns, counts, levels),
        8 << 20,
        1 << 20,
    )

    def prepare(level, store, held):
        return call(
            functools.partial(prepare_level, level, rows, width_k, owners),
            f"prepare_{level}",
            (
                jax.ShapeDtypeStruct(held.shape, held.dtype),
                jax.ShapeDtypeStruct((MEMBERS, *block), jnp.float32),
                jax.ShapeDtypeStruct((MEMBERS, 1 + READY, *tile), jnp.bfloat16),
                jax.ShapeDtypeStruct((MEMBERS,), jnp.int32),
            ),
            (vmem(), vmem(), vmem(), smem()),
            [smem()] * 3 + [vmem()] + [anywhere()] * (2 * MEMBERS + (1 if level else 0)),
            [
                pltpu.VMEM((RING, *tile), jnp.bfloat16),
                pltpu.VMEM((RING, *block), jnp.bfloat16),
                pltpu.SemaphoreType.DMA((RING,)),
                pltpu.SemaphoreType.DMA((RING,)),
                pltpu.SemaphoreType.DMA((MEMBERS * (1 + READY),)),
            ],
            (levels, edges, starts, held, *((store,) if level else ()), *tiles, *inverses),
            32 << 20,
            1 << 20,
        )

    def solve(level, received, store, totals, ready, info):
        last = level == LEVELS - 1
        held_store = (store,) if 1 < level and not last else ()
        operands = (edges, starts, info, totals, ready, received, *tiles, *held_store)
        extra = MEMBERS * (width_k - READY)
        return pl.pallas_call(
            functools.partial(solve_level, level, width_k, owners),
            out_shape=(piece_shape,) if last else (piece_shape, spread_shape, store_shape),
            in_specs=[smem()] * 3 + [vmem()] * 3 + [anywhere()] * (MEMBERS + len(held_store)),
            out_specs=(vmem(),) if last else (vmem(), anywhere(), anywhere()),
            scratch_shapes=[
                pltpu.VMEM((extra, *tile), jnp.bfloat16),
                pltpu.SemaphoreType.DMA((extra,)),
            ]
            + ([] if last else [pltpu.SemaphoreType.DMA((1,)), *fan]),
            input_output_aliases={len(operands) - 1: 2} if held_store else {},
            compiler_params=pltpu.CompilerParams(vmem_limit_bytes=GRANT),
            cost_estimate=pl.CostEstimate(
                flops=4 << 20, bytes_accessed=1 << 18, transcendentals=0
            ),
            name=f"solve_{level}",
        )(*operands)

    def collect(base, befores, pieces):
        return call(
            functools.partial(collect_rows, rows, owners, base),
            "collect_rows",
            (jax.ShapeDtypeStruct((rows, *block), jnp.bfloat16),) * MEMBERS,
            (vmem(),) * MEMBERS,
            [smem()] + [vmem()] * (len(befores) + len(pieces)),
            [],
            (levels, *befores, *pieces),
            1 << 10,
            1 << 18,
        )

    store = None
    for level in range(1, LEVELS):
        held, totals, ready, info = prepare(level - 1, store, held)
        if level == LEVELS - 1:
            early = collect(0, (), pieces)
        piece, *more = solve(level, arriving, store, totals, ready, info)
        if more:
            spread, store = more
            pieces.append(piece)
            arriving = exchanged(spread)

    mine, theirs = collect(LEVELS - 1, early, (piece,))
    theirs = swapped(theirs)
    both = jnp.concatenate([mine, theirs], 1)
    crossed = jnp.concatenate([theirs, mine], 1)
    return jnp.swapaxes(jnp.where(core == 0, both, crossed), 1, 2)[:, None]


def solution(mesh):
    finer = Mesh(mesh.devices.reshape(4, 4, 4, 2), ROWS)
    return jax.shard_map(
        local,
        mesh=finer,
        in_specs=(
            P(None, ROWS, None, None),
            P(None, ROWS, None, None, None),
            P(None, ROWS, None, None),
            P(None, ROWS, None),
            P(None, ROWS),
            P(),
        ),
        out_specs=P(None, ROWS, None, None),
        check_vma=False,
    )
```

```python
import functools

import jax
import jax.numpy as jnp
from jax import lax
from jax.experimental import pallas as pl
from jax.experimental.pallas import tpu as pltpu
from jax.sharding import Mesh
from jax.sharding import PartitionSpec as P

LEVELS = 16
ROWS = ("rows_0", "rows_1", "rows_2", "rows_3")
CHIPS = ("rows_0", "rows_1", "rows_2")
CORE = "rows_3"
SWAP = ((0, 1), (1, 0))
MEMBERS = 2
KEYS = LEVELS * 2 * MEMBERS
RING = 8
FAN = 8
KEPT = 16
GROUP = 3
READY = 6
GRANT = 50 << 20


def smem():
    return pl.BlockSpec(memory_space=pltpu.SMEM)


def vmem():
    return pl.BlockSpec(memory_space=pltpu.VMEM)


def anywhere():
    return pl.BlockSpec(memory_space=pltpu.HBM)


def bucket(level, urgent, member):
    return (level * 2 + (0 if urgent else 1)) * MEMBERS + member


def times_transposed(rows, tile):
    return lax.dot_general(
        rows, tile, (((1,), (1,)), ((), ())), preferred_element_type=jnp.float32
    )


def device_of(member, owners_index):
    core = lax.axis_index(CORE)
    return owners_index + (1 - 2 * core) * member


def slot_of(member):
    core = lax.axis_index(CORE)
    return core if member == 0 else 1 - core


def find_row(levels, owners, member, rows, level):
    own = device_of(member, lax.axis_index(ROWS))
    pick = jnp.int32(-1)
    for s in range(rows):
        pick = jnp.where(levels[s * owners + own] == level, s, pick)
    return pick


def list_edges(owners, columns, counts, levels, edges, starts, fill):
    rows = counts.shape[0] // MEMBERS
    width_k = columns.shape[0] // counts.shape[0]

    def clear(key, unused):
        fill[key] = 0
        return unused

    lax.fori_loop(0, KEYS, clear, 0)

    def over_slots(visit):
        for member in range(MEMBERS):
            own = device_of(member, lax.axis_index(ROWS))

            def each_row(row, unused, member=member, own=own):
                next_level = levels[row * owners + own]
                at = member * rows + row

                def each_slot(slot, unused):
                    col = columns[at * width_k + slot]
                    level = levels[col]
                    late = jnp.where(next_level == level + 1, 0, 1)
                    visit(at * width_k + slot, col, (level * 2 + late) * MEMBERS + member)
                    return unused

                return lax.fori_loop(0, counts[at], each_slot, unused)

            lax.fori_loop(0, rows, each_row, 0)

    def count(slot, col, key):
        fill[key] = fill[key] + 1

    over_slots(count)

    def prefix(key, total):
        starts[key] = total
        here = fill[key]
        fill[key] = total
        return total + here

    starts[KEYS] = lax.fori_loop(0, KEYS, prefix, 0)

    def place(slot, col, key):
        at = fill[key]
        edges[at] = slot * owners + lax.rem(col, owners)
        fill[key] = at + 1

    over_slots(place)


def spread_slot(member, piece, spread, fan, sems):
    at = slot_of(member)
    value = piece[at]
    for i in range(FAN):
        fan[member, i] = value
    copies = [
        pltpu.make_async_copy(
            fan.at[member], spread.at[pl.ds(i * FAN, FAN), at], sems.at[member, i]
        )
        for i in range(spread.shape[0] // FAN)
    ]
    for copy in copies:
        copy.start()
    return copies


def solve_first(rows, owners, levels, held, own_inverse, their_inverse, piece, spread, buf, sems, fan, fan_sems):
    inverses = (own_inverse, their_inverse)
    picks = [find_row(levels, owners, member, rows, 0) for member in range(MEMBERS)]

    def copy(member):
        return pltpu.make_async_copy(
            inverses[member].at[jnp.maximum(picks[member], 0)], buf.at[member], sems.at[member]
        )

    copies = []
    for member in range(MEMBERS):
        copy(member).start()
    for member in range(MEMBERS):
        at = slot_of(member)
        copy(member).wait()
        row = held[member * rows + jnp.maximum(picks[member], 0)].astype(jnp.bfloat16)
        solved = times_transposed(row, buf[member])
        piece[at] = jnp.where(picks[member] >= 0, solved, 0.0).astype(jnp.bfloat16)
        copies += spread_slot(member, piece, spread, fan, fan_sems)
    for spreading in copies:
        spreading.wait()


def prepare_level(level, rows, width_k, owners, levels, edges, starts, held_in, *refs):
    if level:
        store, *refs = refs
    tiles, inverses = refs[:MEMBERS], refs[MEMBERS : 2 * MEMBERS]
    held, totals, ready, info, buf, blocks, sems, block_sems, ready_sems = refs[2 * MEMBERS :]
    slots = 1 + READY
    picks = [find_row(levels, owners, member, rows, level + 1) for member in range(MEMBERS)]

    def tile_of(member, i):
        code = edges[i] // owners - member * rows * width_k
        return tiles[member].at[code // width_k, lax.rem(code, width_k)]

    def ready_copy(member, place, source):
        return pltpu.make_async_copy(
            source, ready.at[member, place], ready_sems.at[member * slots + place]
        )

    def late_copy(member, first, i):
        at = lax.rem(i, RING)
        return pltpu.make_async_copy(tile_of(member, first + i), buf.at[at], sems.at[at])

    def block_copy(first, i):
        at = lax.rem(i, RING)
        return pltpu.make_async_copy(
            store.at[(level - 1) // 2, first + i], blocks.at[at], block_sems.at[at]
        )

    late = []
    if level:
        for member in range(MEMBERS):
            key = bucket(level - 1, False, member)
            late.append((starts[key], starts[key + 1] - starts[key]))
        first, many = late[0]

        def begin(i, unused, first=first):
            late_copy(0, first, i).start()
            block_copy(first, i).start()
            return unused

        lax.fori_loop(0, jnp.minimum(many, RING), begin, 0)

    urgent = []
    for member in range(MEMBERS):
        key = bucket(level, True, member)
        first, many = starts[key], starts[key + 1] - starts[key]
        urgent.append(jnp.minimum(many, READY))
        info[member] = jnp.where(picks[member] >= 0, many, 0)
        ready_copy(member, 0, inverses[member].at[jnp.maximum(picks[member], 0)]).start()

        def fetch(i, unused, member=member, first=first):
            ready_copy(member, 1 + i, tile_of(member, first + i)).start()
            return unused

        lax.fori_loop(0, urgent[member], fetch, 0)

    held[...] = held_in[...]
    if level:
        for member in range(MEMBERS):
            first, many = late[member]
            if member:

                def begin(i, unused, member=member, first=first):
                    late_copy(member, first, i).start()
                    block_copy(first, i).start()
                    return unused

                lax.fori_loop(0, jnp.minimum(many, RING), begin, 0)

            def absorb(i, unused, member=member, first=first, many=many):
                late_copy(member, first, i).wait()
                block_copy(first, i).wait()
                row = edges[first + i] // (owners * width_k)
                at = lax.rem(i, RING)
                given = times_transposed(blocks[at], buf[at])
                held[row] = held[row] - given

                @pl.when(i + RING < many)
                def _():
                    late_copy(member, first, i + RING).start()
                    block_copy(first, i + RING).start()

                return unused

            lax.fori_loop(0, many, absorb, 0)

    for member in range(MEMBERS):
        totals[member] = held[member * rows + jnp.maximum(picks[member], 0)]
        ready_copy(member, 0, inverses[member].at[0]).wait()

        def settle(i, unused, member=member):
            ready_copy(member, 1 + i, tiles[member].at[0, 0]).wait()
            return unused

        lax.fori_loop(0, urgent[member], settle, 0)


def solve_level(level, width_k, owners, edges, starts, info, totals, ready, received, *refs):
    tiles, refs = refs[:MEMBERS], refs[MEMBERS:]
    last = level == LEVELS - 1
    if last:
        piece, buf, sems = refs
    else:
        piece, spread, store, buf, sems, keep_sem, *fan = refs[1 if level > 1 else 0 :]

        def keep_copy(edge):
            return pltpu.make_async_copy(
                received.at[lax.rem(edges[edge], owners)],
                store.at[(level - 1) // 2, edge],
                keep_sem.at[lax.rem(edge, KEPT)],
            )

    copies = []
    extra = width_k - READY

    def extra_copy(member, i):
        code = edges[starts[bucket(level - 1, True, member)] + i] // owners
        code = code - member * tiles[member].shape[0] * width_k
        at = member * extra + i - READY
        return pltpu.make_async_copy(
            tiles[member].at[code // width_k, lax.rem(code, width_k)], buf.at[at], sems.at[at]
        )

    for member in range(MEMBERS):

        def begin(i, unused, member=member):
            extra_copy(member, i).start()
            return unused

        lax.fori_loop(READY, info[member], begin, 0)

    for member in range(MEMBERS):
        at = slot_of(member)
        many = info[member]

        @pl.when(many == 0)
        def _(at=at):
            piece[at] = jnp.zeros(piece.shape[1:], piece.dtype)

        @pl.when(many > 0)
        def _(member=member, at=at, many=many):
            first = starts[bucket(level - 1, True, member)]
            near = jnp.minimum(many, READY)

            def absorb(group, total):
                for u in range(GROUP):
                    i = group * GROUP + u
                    here = jnp.minimum(i, near - 1)
                    block = received[lax.rem(edges[first + here], owners)]
                    block = jnp.where(i < near, block, jnp.zeros_like(block))
                    total = total - times_transposed(block, ready[member, 1 + here])
                return total

            def absorb_extra(i, total):
                extra_copy(member, i).wait()
                block = received[lax.rem(edges[first + i], owners)]
                return total - times_transposed(block, buf[member * extra + i - READY])

            total = lax.fori_loop(0, (near + GROUP - 1) // GROUP, absorb, totals[member])
            total = lax.fori_loop(READY, many, absorb_extra, total)
            solved = times_transposed(total.astype(jnp.bfloat16), ready[member, 0])
            piece[at] = solved.astype(jnp.bfloat16)

        if not last:
            copies += spread_slot(member, piece, spread, *fan)

    if not last:
        first_kept = starts[bucket(level - 1, False, 0)]
        end_kept = starts[bucket(level - 1, False, MEMBERS - 1) + 1]

        def keep(edge, unused):
            @pl.when(edge - KEPT >= first_kept)
            def _():
                keep_copy(edge - KEPT).wait()

            keep_copy(edge).start()
            return unused

        def kept(edge, unused):
            keep_copy(edge).wait()
            return unused

        lax.fori_loop(first_kept, end_kept, keep, 0)
        lax.fori_loop(jnp.maximum(first_kept, end_kept - KEPT), end_kept, kept, 0)
        for copy in copies:
            copy.wait()


def collect_rows(rows, owners, base, levels, *refs):
    pieces, outs = refs[:-MEMBERS], refs[-MEMBERS:]
    if base:
        befores, pieces = pieces[:MEMBERS], pieces[MEMBERS:]
    for member in range(MEMBERS):
        if base:
            outs[member][...] = befores[member][...]
        for i, piece in enumerate(pieces):
            row = find_row(levels, owners, member, rows, base + i)

            @pl.when(row >= 0)
            def _(piece=piece, member=member, row=row):
                outs[member][row] = piece[slot_of(member)]


def local(right_sides, lower_tiles, diag_inverse, tile_columns, tile_counts, level_sets):
    owners = lax.axis_size(ROWS)
    chips = lax.axis_size(CHIPS)
    core = lax.axis_index(CORE)
    rows, unused_one, width_k = tile_columns.shape
    part = right_sides.shape[3] // MEMBERS
    lanes = right_sides.shape[2]
    block = (part, lanes)
    tile = lower_tiles.shape[3:]

    def swapped(value):
        return lax.ppermute(value, CORE, SWAP)

    levels = level_sets.reshape(-1)
    rhs = jnp.swapaxes(right_sides[:, 0], 1, 2)
    rhs_mine = lax.dynamic_slice_in_dim(rhs, core * part, part, 1)
    rhs_theirs = swapped(lax.dynamic_slice_in_dim(rhs, (1 - core) * part, part, 1))
    held = jnp.concatenate([rhs_mine, rhs_theirs])
    inverses = (diag_inverse[:, 0], swapped(diag_inverse[:, 0]))

    def call(kernel, name, out_shape, out_specs, in_specs, scratch, operands, flops, moved):
        return pl.pallas_call(
            kernel,
            out_shape=out_shape,
            in_specs=in_specs,
            out_specs=out_specs,
            scratch_shapes=scratch,
            compiler_params=pltpu.CompilerParams(vmem_limit_bytes=GRANT),
            cost_estimate=pl.CostEstimate(flops=flops, bytes_accessed=moved, transcendentals=0),
            name=name,
        )(*operands)

    piece_shape = jax.ShapeDtypeStruct((MEMBERS, *block), jnp.bfloat16)
    spread_shape = jax.ShapeDtypeStruct((chips, MEMBERS, *block), jnp.bfloat16)

    store_shape = jax.ShapeDtypeStruct(
        ((LEVELS - 1) // 2, MEMBERS * rows * width_k, *block), jnp.bfloat16
    )

    fan = [
        pltpu.VMEM((MEMBERS, FAN, *block), jnp.bfloat16),
        pltpu.SemaphoreType.DMA((MEMBERS, chips // FAN)),
    ]

    def exchanged(spread):
        return lax.all_to_all(spread, CHIPS, 0, 0, tiled=True).reshape(owners, *block)

    piece, spread = call(
        functools.partial(solve_first, rows, owners),
        "solve_0",
        (piece_shape, spread_shape),
        (vmem(), anywhere()),
        [smem(), vmem(), anywhere(), anywhere()],
        [pltpu.VMEM((MEMBERS, *tile), jnp.bfloat16), pltpu.SemaphoreType.DMA((MEMBERS,)), *fan],
        (levels, held, *inverses),
        4 << 20,
        1 << 18,
    )
    pieces = [piece]
    arriving = exchanged(spread)

    own_tiles, columns_own, counts_own, unused_tie = lax.optimization_barrier(
        (lower_tiles[:, 0], tile_columns[:, 0], tile_counts[:, 0], piece)
    )
    tiles = (own_tiles, swapped(own_tiles))
    columns = jnp.concatenate([columns_own, swapped(columns_own)]).reshape(-1)
    counts = jnp.concatenate([counts_own, swapped(counts_own)])
    edges, starts = call(
        functools.partial(list_edges, owners),
        "list_edges",
        (
            jax.ShapeDtypeStruct((columns.size,), jnp.int32),
            jax.ShapeDtypeStruct((KEYS + 1,), jnp.int32),
        ),
        (smem(), smem()),
        [smem()] * 3,
        [pltpu.SMEM((KEYS,), jnp.int32)],
        (columns, counts, levels),
        8 << 20,
        1 << 20,
    )

    def prepare(level, store, held):
        return call(
            functools.partial(prepare_level, level, rows, width_k, owners),
            f"prepare_{level}",
            (
                jax.ShapeDtypeStruct(held.shape, held.dtype),
                jax.ShapeDtypeStruct((MEMBERS, *block), jnp.float32),
                jax.ShapeDtypeStruct((MEMBERS, 1 + READY, *tile), jnp.bfloat16),
                jax.ShapeDtypeStruct((MEMBERS,), jnp.int32),
            ),
            (vmem(), vmem(), vmem(), smem()),
            [smem()] * 3 + [vmem()] + [anywhere()] * (2 * MEMBERS + (1 if level else 0)),
            [
                pltpu.VMEM((RING, *tile), jnp.bfloat16),
                pltpu.VMEM((RING, *block), jnp.bfloat16),
                pltpu.SemaphoreType.DMA((RING,)),
                pltpu.SemaphoreType.DMA((RING,)),
                pltpu.SemaphoreType.DMA((MEMBERS * (1 + READY),)),
            ],
            (levels, edges, starts, held, *((store,) if level else ()), *tiles, *inverses),
            32 << 20,
            1 << 20,
        )

    def solve(level, received, store, totals, ready, info):
        last = level == LEVELS - 1
        held_store = (store,) if 1 < level and not last else ()
        operands = (edges, starts, info, totals, ready, received, *tiles, *held_store)
        extra = MEMBERS * (width_k - READY)
        return pl.pallas_call(
            functools.partial(solve_level, level, width_k, owners),
            out_shape=(piece_shape,) if last else (piece_shape, spread_shape, store_shape),
            in_specs=[smem()] * 3 + [vmem()] * 3 + [anywhere()] * (MEMBERS + len(held_store)),
            out_specs=(vmem(),) if last else (vmem(), anywhere(), anywhere()),
            scratch_shapes=[
                pltpu.VMEM((extra, *tile), jnp.bfloat16),
                pltpu.SemaphoreType.DMA((extra,)),
            ]
            + ([] if last else [pltpu.SemaphoreType.DMA((KEPT,)), *fan]),
            input_output_aliases={len(operands) - 1: 2} if held_store else {},
            compiler_params=pltpu.CompilerParams(vmem_limit_bytes=GRANT),
            cost_estimate=pl.CostEstimate(
                flops=4 << 20, bytes_accessed=1 << 18, transcendentals=0
            ),
            name=f"solve_{level}",
        )(*operands)

    def collect(base, befores, pieces):
        return call(
            functools.partial(collect_rows, rows, owners, base),
            "collect_rows",
            (jax.ShapeDtypeStruct((rows, *block), jnp.bfloat16),) * MEMBERS,
            (vmem(),) * MEMBERS,
            [smem()] + [vmem()] * (len(befores) + len(pieces)),
            [],
            (levels, *befores, *pieces),
            1 << 10,
            1 << 18,
        )

    store = None
    for level in range(1, LEVELS):
        held, totals, ready, info = prepare(level - 1, store, held)
        if level == LEVELS - 1:
            early = collect(0, (), pieces)
        piece, *more = solve(level, arriving, store, totals, ready, info)
        if more:
            spread, store = more
            pieces.append(piece)
            arriving = exchanged(spread)

    mine, theirs = collect(LEVELS - 1, early, (piece,))
    theirs = swapped(theirs)
    both = jnp.concatenate([mine, theirs], 1)
    crossed = jnp.concatenate([theirs, mine], 1)
    return jnp.swapaxes(jnp.where(core == 0, both, crossed), 1, 2)[:, None]


def solution(mesh):
    finer = Mesh(mesh.devices.reshape(4, 4, 4, 2), ROWS)
    return jax.shard_map(
        local,
        mesh=finer,
        in_specs=(
            P(None, ROWS, None, None),
            P(None, ROWS, None, None, None),
            P(None, ROWS, None, None),
            P(None, ROWS, None),
            P(None, ROWS),
            P(),
        ),
        out_specs=P(None, ROWS, None, None),
        check_vma=False,
    )
```
